128 devices in a mesh: dp: 32 (over y, z_hi, x), row: 2 (over z_lo), col: 2 (over core).
Axes of the slice: x: 4, y: 4, z: 4 (z_hi: 2, z_lo: 2; z = z_hi * 2 + z_lo), core: 2. Of those that a mesh axis runs over, the one named last changes fastest.
Arguments:
- features: bfloat16 [32, 8, 64, 2048], P('dp', 'row', 'col'), may hold values from -6 to 6
- cotangent: bfloat16 [32, 8, 64, 2048], P('dp', 'row', 'col'), may hold values from -6 to 6
- kernel_one: float32 [4, 512, 1152], P(('row', 'col'), 'dp'), may hold values from -0.1875 to 0.1875
- kernel_two: float32 [4, 512, 1152], P(('row', 'col'), 'dp'), may hold values from -0.1875 to 0.1875
- gain_one: float32 [4, 512], P(('row', 'col'), 'dp'), may hold values from 0.5 to 1.5
- gain_two: float32 [4, 512], P(('row', 'col'), 'dp'), may hold values from 0.5 to 1.5
Outputs:
- outputs: bfloat16 [32, 8, 64, 2048], P('dp', 'row', 'col')
- input_grad: bfloat16 [32, 8, 64, 2048], P('dp', 'row', 'col')
- kernel_grad_one: float32 [4, 512, 1152], P(('row', 'col'), 'dp')
- kernel_grad_two: float32 [4, 512, 1152], P(('row', 'col'), 'dp')
The draws below stay inside these ranges and needn't reach their ends.
All inputs are finite; a program needn't handle non-finite values.
Results may differ from the reference program's by a relative error of at most 0.028.
Values may be sent and summed in bfloat16 or wider, within the bound.
A program may use at most 128 MiB of HBM per device.

```python
import math
import jax
import jax.numpy as jnp
from jax import lax

C = 2048
GROUP = 128
IMAGES = 32
HEIGHT = 8
WIDTH = 64
BLOCKS = 4


def shard_levels(key, shape, pieces, least, top_value):
    loudness = 1.0
    for position, blocks in pieces:
        draws = jax.random.uniform(jax.random.fold_in(jax.random.fold_in(key, 6), position), (blocks,), jnp.float32, least / len(pieces), top_value / len(pieces))
        loudness = loudness * jnp.repeat(jnp.exp(draws), shape[position] // blocks).reshape((-1,) + (1,) * (len(shape) - 1 - position))
    return loudness


def bell_draw(stream_key, dims, scale, most, pieces=(), kind=jnp.bfloat16):
    level = shard_levels(stream_key, dims, pieces, -0.22, 0.18) if pieces else 1.0
    drawn = jax.random.normal(stream_key, dims, jnp.float32) * scale * level
    return jnp.minimum(jnp.maximum(drawn, -most), most).astype(kind)


def setup_inputs(seed: int = 0) -> dict:
    splits = jax.random.split(jax.random.key(seed), 7)
    features = bell_draw(splits[0], (IMAGES, HEIGHT, WIDTH, C), 1.0, 6.0, ((0, 32), (1, 2), (2, 2)))
    cotangent = bell_draw(splits[1], (IMAGES, HEIGHT, WIDTH, C), 1.0, 6.0, ((0, 32), (1, 2), (2, 2)))
    kernel_one = bell_draw(splits[2], (BLOCKS, C // BLOCKS, 9 * GROUP), (9 * GROUP) ** -0.5, 0.1875, ((0, 4), (1, 32)), jnp.float32)
    kernel_two = bell_draw(splits[3], (BLOCKS, C // BLOCKS, 9 * GROUP), (9 * GROUP) ** -0.5, 0.1875, ((0, 4), (1, 32)), jnp.float32)
    gain_one = jnp.clip(1.0 + 0.1 * jax.random.normal(splits[4], (BLOCKS, C // BLOCKS), jnp.float32), 0.5, 1.5)
    gain_two = jnp.clip(1.0 + 0.1 * jax.random.normal(splits[5], (BLOCKS, C // BLOCKS), jnp.float32), 0.5, 1.5)
    return dict(features=features, cotangent=cotangent, kernel_one=kernel_one, kernel_two=kernel_two, gain_one=gain_one, gain_two=gain_two)


GAMMA = 1.7015043497085571
ALPHA = 0.2
EPS = 1e-06

def activate(value):
    return jax.nn.gelu(value, approximate=True) * GAMMA

def act_pull(value, grad):
    _, pull = jax.vjp(activate, value)
    return pull(grad)[0]

def standardize(kernel, gain):
    mean = lax.optimization_barrier(jnp.mean(kernel, axis=-1, keepdims=True))
    centered = kernel - mean
    spread = lax.optimization_barrier(jnp.mean(centered * centered, axis=-1, keepdims=True))
    return gain[..., None] * centered * lax.rsqrt(spread + EPS) / math.sqrt(kernel.shape[-1])

def conv_forward(padded, kernel, group):
    images, hp, wp, chans = padded.shape
    height, width, groups = (hp - 2, wp - 2, chans // group)
    kern = kernel.astype(jnp.float32).reshape(groups, group, 9, group)
    total = jnp.zeros((images, height, width, groups, group), jnp.float32)
    for tap in range(9):
        row_off, col_off = (tap // 3, tap % 3)
        piece = padded[:, row_off:row_off + height, col_off:col_off + width, :].astype(jnp.float32)
        piece = piece.reshape(images, height, width, groups, group)
        total = total + jnp.einsum('bhwgi,goi->bhwgo', piece, kern[:, :, tap, :], precision=lax.Precision.HIGHEST)
    return total.reshape(images, height, width, chans)

def conv_adjoint(padded, kernel, group):
    images, hp, wp, chans = padded.shape
    height, width, groups = (hp - 2, wp - 2, chans // group)
    kern = kernel.astype(jnp.float32).reshape(groups, group, 9, group)
    total = jnp.zeros((images, height, width, groups, group), jnp.float32)
    for tap in range(9):
        row_off, col_off = (tap // 3, tap % 3)
        piece = padded[:, 2 - row_off:2 - row_off + height, 2 - col_off:2 - col_off + width, :].astype(jnp.float32)
        piece = piece.reshape(images, height, width, groups, group)
        total = total + jnp.einsum('bhwgo,goi->bhwgi', piece, kern[:, :, tap, :], precision=lax.Precision.HIGHEST)
    return total.reshape(images, height, width, chans)

def kernel_terms(grad_out, padded, group):
    images, height, width, chans = grad_out.shape
    groups = chans // group
    upper = grad_out.astype(jnp.float32).reshape(images, height, width, groups, group)
    terms = []
    for tap in range(9):
        row_off, col_off = (tap // 3, tap % 3)
        piece = padded[:, row_off:row_off + height, col_off:col_off + width, :].astype(jnp.float32)
        piece = piece.reshape(images, height, width, groups, group)
        terms.append(jnp.einsum('bhwgo,bhwgi->goi', upper, piece, precision=lax.Precision.HIGHEST))
    return jnp.stack(terms, axis=2).reshape(chans, 9 * group)

def pad_map(value):
    return jnp.pad(value, ((0, 0), (1, 1), (1, 1), (0, 0)))

def reference(features, cotangent, kernel_one, kernel_two, gain_one, gain_two):
    blocks, block_rows, fan = kernel_one.shape
    chans = blocks * block_rows
    flat_one = kernel_one.reshape(chans, fan)
    flat_two = kernel_two.reshape(chans, fan)
    gains_one = gain_one.reshape(chans)
    gains_two = gain_two.reshape(chans)
    w_one = standardize(flat_one, gains_one).astype(jnp.bfloat16)
    w_two = standardize(flat_two, gains_two).astype(jnp.bfloat16)

    def one_image(carry, pair):
        image, grad_image = pair
        image = image[None]
        grad_image = grad_image[None]
        first = activate(image.astype(jnp.float32)).astype(jnp.bfloat16)
        pad_first = pad_map(first)
        hidden_pre = conv_forward(pad_first, w_one, GROUP).astype(jnp.bfloat16)
        hidden = activate(hidden_pre.astype(jnp.float32)).astype(jnp.bfloat16)
        pad_hidden = pad_map(hidden)
        result = (image.astype(jnp.float32) + ALPHA * conv_forward(pad_hidden, w_two, GROUP)).astype(jnp.bfloat16)
        upper = (ALPHA * grad_image.astype(jnp.float32)).astype(jnp.bfloat16)
        hidden_grad = conv_adjoint(pad_map(upper), w_two, GROUP)
        lower = act_pull(hidden_pre.astype(jnp.float32), hidden_grad).astype(jnp.bfloat16)
        back = conv_adjoint(pad_map(lower), w_one, GROUP)
        in_grad = (grad_image.astype(jnp.float32) + act_pull(image.astype(jnp.float32), back)).astype(jnp.bfloat16)
        sum_one = carry[0] + kernel_terms(lower, pad_first, GROUP)
        sum_two = carry[1] + kernel_terms(upper, pad_hidden, GROUP)
        return ((sum_one, sum_two), (result[0], in_grad[0]))
    start = (jnp.zeros((chans, fan), jnp.float32), jnp.zeros((chans, fan), jnp.float32))
    sums, stacked = lax.scan(one_image, start, (features, cotangent))
    _, pull_one = jax.vjp(standardize, flat_one, gains_one)
    _, pull_two = jax.vjp(standardize, flat_two, gains_two)
    grad_one = pull_one(sums[0])[0].reshape(blocks, block_rows, fan)
    grad_two = pull_two(sums[1])[0].reshape(blocks, block_rows, fan)
    return (stacked[0], stacked[1], grad_one, grad_two)
```

```python
import functools
import math

import jax
import jax.numpy as jnp
from jax import lax
from jax.experimental import pallas as pl
from jax.experimental.pallas import tpu as pltpu
from jax.sharding import PartitionSpec as P

MESH = pl.DeviceIdType.MESH
GAMMA = 1.7015043497085571
ALPHA = 0.2
EPS = 1e-06
G = 128
FAN = 9 * G
ROOT = math.sqrt(FAN)
NY, NZ, NX = 4, 2, 4
MEMBERS = NZ * NX
H, W = 8, 64
PIX = H * W
BF = jnp.bfloat16
F32 = jnp.float32
CUBE = 0.044715
SLOPE = math.sqrt(2 / math.pi)


def gelu_pair(x):
    square = x * x
    t = jnp.tanh(SLOPE * x * (1.0 + CUBE * square))
    half = (0.5 * GAMMA) * (1.0 + t)
    value = half * x
    slope = half + (0.5 * GAMMA * SLOPE) * x * (1.0 - t * t) * (1.0 + (3.0 * CUBE) * square)
    return value, slope


def column(gain):
    n = gain.shape[1]
    eye = lax.broadcasted_iota(jnp.int32, (n, n), 0) == lax.broadcasted_iota(jnp.int32, (n, n), 1)
    return jnp.sum(jnp.where(eye, jnp.broadcast_to(gain, (n, n)), 0.0), axis=1, keepdims=True)


def centre(kernel):
    c = kernel - jnp.mean(kernel, axis=1, keepdims=True)
    r = lax.rsqrt(jnp.mean(c * c, axis=1, keepdims=True) + EPS)
    return c, r


def body(
    feat, cot, k1, k2, g1, g2,
    out, igrad, kg1, kg2,
    xin, cin, obuf, ibuf, shard, wall, wf, wa, apad, hpad, gpad, zpad, slope_x, slope_z,
    acc, gsend, grecv,
    in_send, in_recv, w_send, w_recv, o_send, o_recv, g_send, g_recv,
):
    dp, row, col = lax.axis_index("dp"), lax.axis_index("row"), lax.axis_index("col")
    y, m = dp // MEMBERS, dp % MEMBERS
    seat = y * 4 + row * 2 + col
    group = (row * 2 + col) * NY + y

    def peer(s):
        s = lax.rem(s, 16)
        py, prow, pcol = s // 4, (s // 2) % 2, s % 2
        return (py * MEMBERS + m, prow, pcol), py, prow, pcol

    def mate(j):
        pm = lax.rem(m + j, MEMBERS)
        return (y * MEMBERS + pm, row, col), pm

    barrier = pltpu.get_barrier_semaphore()

    @pl.loop(1, 16)
    def _(k):
        pl.semaphore_signal(barrier, inc=1, device_id=peer(seat + k)[0], device_id_type=MESH)

    @pl.loop(1, MEMBERS)
    def _(j):
        pl.semaphore_signal(barrier, inc=1, device_id=mate(j)[0], device_id_type=MESH)

    gains = (column(g1[...]), column(g2[...]))
    for idx, k in enumerate((k1, k2)):
        c, r = centre(k[0])
        shard[idx] = (gains[idx] * c * r / ROOT).astype(BF)
    zero = jnp.zeros((W, G), BF)
    for pad in (apad, hpad, gpad, zpad):
        pad[0:W] = zero
        pad[W + PIX : 2 * W + PIX] = zero
    acc[...] = jnp.zeros_like(acc)

    pl.semaphore_wait(barrier, 15 + MEMBERS - 1)

    def in_copy(which, k):
        src, dst = ((feat, xin), (cot, cin))[which]
        dev, py, prow, pcol = peer(seat + k)
        lane = pl.multiple_of(((prow * 2 + pcol) * NY + py) * G, G)
        s = src.at[0, :, :, pl.ds(lane, G)]
        d = dst.at[y, pl.ds(row * 4, 4), pl.ds(pl.multiple_of(col * 32, 32), 32), :]
        return s, d, dev

    def w_copy(j):
        dev, _ = mate(j)
        return pltpu.make_async_remote_copy(
            src_ref=shard, dst_ref=wall.at[:, pl.ds(pl.multiple_of(m * 16, 16), 16), :],
            send_sem=w_send.at[j], recv_sem=w_recv, device_id=dev, device_id_type=MESH,
        )

    def in_remote(which, k):
        s, d, dev = in_copy(which, k)
        return pltpu.make_async_remote_copy(
            src_ref=s, dst_ref=d, send_sem=in_send.at[which, k], recv_sem=in_recv.at[which, y],
            device_id=dev, device_id_type=MESH,
        )

    def own_copy(which):
        s, d, _ = in_copy(which, 0)
        return pltpu.make_async_copy(s, d, in_recv.at[which, y])

    def own_shard():
        return pltpu.make_async_copy(
            shard, wall.at[:, pl.ds(pl.multiple_of(m * 16, 16), 16), :], w_recv
        )

    own_copy(0).start()
    own_copy(1).start()

    @pl.loop(1, MEMBERS)
    def _(j):
        w_copy(j).start()

    own_shard().start()

    @pl.loop(1, 16)
    def _(k):
        in_remote(0, k).start()
        in_remote(1, k).start()

    pltpu.make_async_copy(wall, wall, w_recv).wait()
    for idx in range(2):
        for dy in range(3):
            wa[idx, dy * G : (dy + 1) * G, :] = wall[idx, :, 3 * G * dy : 3 * G * (dy + 1)]
            for dx in range(3):
                wf[idx, dx * G : (dx + 1) * G, dy * G : (dy + 1) * G] = wall[
                    idx, :, (3 * dy + dx) * G : (3 * dy + dx + 1) * G
                ]

    where = lax.broadcasted_iota(jnp.int32, (PIX, G), 0) % W
    first, last = where == 0, where == W - 1

    def later(v):
        return jnp.where(first, 0.0, pltpu.roll(v, 1, 0))

    def sooner(v):
        return jnp.where(last, 0.0, pltpu.roll(v, PIX - 1, 0))

    def stack(pad, order):
        return jnp.concatenate([pad[d * W : d * W + PIX] for d in order], axis=1)

    def forward(pad, idx):
        p = lax.dot_general(
            stack(pad, (0, 1, 2)), wf[idx], (((1,), (1,)), ((), ())), preferred_element_type=F32
        )
        return later(p[:, :G]) + p[:, G : 2 * G] + sooner(p[:, 2 * G :])

    def adjoint(pad, idx):
        p = jnp.dot(stack(pad, (2, 1, 0)), wa[idx], preferred_element_type=F32)
        return sooner(p[:, :G]) + p[:, G : 2 * G] + later(p[:, 2 * G :])

    def terms(v, pad, idx):
        g = jnp.concatenate([sooner(v).astype(BF), v.astype(BF), later(v).astype(BF)], axis=1)
        acc[idx] += lax.dot_general(
            g, stack(pad, (0, 1, 2)), (((0,), (0,)), ((), ())), preferred_element_type=F32
        )

    def out_remote(which, n, p):
        src, dst = ((obuf, out), (ibuf, igrad))[which]
        prow, pcol = p // 2, p % 2
        s = src.at[n, pl.ds(prow * 4, 4), pl.ds(pl.multiple_of(pcol * 32, 32), 32), :]
        d = dst.at[0, :, :, pl.ds(pl.multiple_of(group * G, G), G)]
        return s, d, (n * MEMBERS + m, prow, pcol), n * 4 + p

    def out_start(which, n):
        @pl.loop(0, 4)
        def _(p):
            s, d, dev, slot = out_remote(which, n, p)
            mine = slot == seat

            @pl.when(mine)
            def _():
                pltpu.make_async_copy(s, d, o_recv.at[which]).start()

            @pl.when(jnp.logical_not(mine))
            def _():
                pltpu.make_async_remote_copy(
                    src_ref=s, dst_ref=d, send_sem=o_send.at[which, slot],
                    recv_sem=o_recv.at[which], device_id=dev, device_id_type=MESH,
                ).start()

    @pl.loop(0, NY)
    def _(j):
        n = lax.rem(y + j + (j // 2) * (5 - 2 * j), NY)
        pltpu.make_async_copy(xin.at[n], xin.at[n], in_recv.at[0, n]).wait()
        x = xin[n].reshape(PIX, G).astype(F32)
        value, slope = gelu_pair(x)
        slope_x[...] = slope
        apad[W : W + PIX] = value.astype(BF)
        z = forward(apad, 0).astype(BF).astype(F32)
        value, slope = gelu_pair(z)
        slope_z[...] = slope
        hpad[W : W + PIX] = value.astype(BF)
        res = xin[n].reshape(PIX, G).astype(F32) + ALPHA * forward(hpad, 1)
        obuf[n] = res.astype(BF).reshape(H, W, G)
        pltpu.make_async_copy(cin.at[n], cin.at[n], in_recv.at[1, n]).wait()
        c = cin[n].reshape(PIX, G).astype(F32)
        upper = (ALPHA * c).astype(BF)
        gpad[W : W + PIX] = upper
        lower = (adjoint(gpad, 1) * slope_z[...]).astype(BF)
        zpad[W : W + PIX] = lower
        out_start(0, n)
        back = adjoint(zpad, 0)
        ig = cin[n].reshape(PIX, G).astype(F32) + slope_x[...] * back
        ibuf[n] = ig.astype(BF).reshape(H, W, G)
        terms(gpad[W : W + PIX].astype(F32), hpad, 1)
        terms(zpad[W : W + PIX].astype(F32), apad, 0)
        out_start(1, n)

    for idx in range(2):
        for dy in range(3):
            for dx in range(3):
                gsend[idx, :, (3 * dy + dx) * G : (3 * dy + dx + 1) * G] = acc[
                    idx, dx * G : (dx + 1) * G, dy * G : (dy + 1) * G
                ].astype(BF)

    def g_copy(j):
        dev, pm = mate(j)
        return pltpu.make_async_remote_copy(
            src_ref=gsend.at[:, pl.ds(pl.multiple_of(pm * 16, 16), 16), :],
            dst_ref=grecv.at[m], send_sem=g_send.at[j], recv_sem=g_recv,
            device_id=dev, device_id_type=MESH,
        )

    def own_grad():
        return pltpu.make_async_copy(
            gsend.at[:, pl.ds(pl.multiple_of(m * 16, 16), 16), :], grecv.at[m], g_recv
        )

    @pl.loop(1, MEMBERS)
    def _(j):
        g_copy(j).start()

    own_grad().start()

    @pl.loop(1, 16)
    def _(k):
        in_remote(0, k).wait_send()
        in_remote(1, k).wait_send()

    @pl.loop(1, MEMBERS)
    def _(j):
        w_copy(j).wait_send()

    pltpu.make_async_copy(grecv, grecv, g_recv).wait()
    for idx, (k, kg) in enumerate(((k1, kg1), (k2, kg2))):
        total = grecv[0, idx].astype(F32)
        for s in range(1, MEMBERS):
            total = total + grecv[s, idx].astype(F32)
        c, r = centre(k[0])
        scale = gains[idx] * r / ROOT
        d = scale * (total - c * (r * r * jnp.mean(total * c, axis=1, keepdims=True)))
        kg[0] = d - jnp.mean(d, axis=1, keepdims=True)

    @pl.loop(1, MEMBERS)
    def _(j):
        g_copy(j).wait_send()

    for which in range(2):
        @pl.loop(0, 16)
        def _(slot):
            @pl.when(slot != seat)
            def _():
                s, d, dev, _ = out_remote(which, slot // 4, slot % 4)
                pltpu.make_async_remote_copy(
                    src_ref=s, dst_ref=d, send_sem=o_send.at[which, slot],
                    recv_sem=o_recv.at[which], device_id=dev, device_id_type=MESH,
                ).wait_send()

        dst = (out, igrad)[which]
        pltpu.make_async_copy(dst, dst, o_recv.at[which]).wait()


def local(features, cotangent, kernel_one, kernel_two, gain_one, gain_two):
    whole = pl.BlockSpec(memory_space=pltpu.VMEM)
    raw = pl.BlockSpec(memory_space=pl.ANY)
    vm = pltpu.VMEM
    dma = pltpu.SemaphoreType.DMA
    return pl.pallas_call(
        body,
        out_shape=(
            jax.ShapeDtypeStruct(features.shape, BF),
            jax.ShapeDtypeStruct(features.shape, BF),
            jax.ShapeDtypeStruct(kernel_one.shape, F32),
            jax.ShapeDtypeStruct(kernel_two.shape, F32),
        ),
        in_specs=[raw, raw, whole, whole, whole, whole],
        out_specs=(raw, raw, whole, whole),
        scratch_shapes=[
            vm((NY, H, W, G), BF), vm((NY, H, W, G), BF),
            vm((NY, H, W, G), BF), vm((NY, H, W, G), BF),
            vm((2, 16, FAN), BF), vm((2, G, FAN), BF),
            vm((2, 3 * G, 3 * G), BF), vm((2, 3 * G, 3 * G), BF),
            vm((PIX + 2 * W, G), BF), vm((PIX + 2 * W, G), BF),
            vm((PIX + 2 * W, G), BF), vm((PIX + 2 * W, G), BF),
            vm((PIX, G), F32), vm((PIX, G), F32),
            vm((2, 3 * G, 3 * G), F32),
            vm((2, G, FAN), BF), vm((MEMBERS, 2, 16, FAN), BF),
            dma((2, 16)), dma((2, NY)), dma((MEMBERS,)), dma,
            dma((2, 16)), dma((2,)), dma((MEMBERS,)), dma,
        ],
        compiler_params=pltpu.CompilerParams(
            collective_id=0, has_side_effects=True, vmem_limit_bytes=48 << 20
        ),
        name="block",
    )(features, cotangent, kernel_one, kernel_two, gain_one, gain_two)


def solution(mesh):
    return jax.shard_map(
        local,
        mesh=mesh,
        in_specs=(
            P("dp", "row", "col", None),
            P("dp", "row", "col", None),
            P(("row", "col"), "dp", None),
            P(("row", "col"), "dp", None),
            P(("row", "col"), "dp"),
            P(("row", "col"), "dp"),
        ),
        out_specs=(
            P("dp", "row", "col", None),
            P("dp", "row", "col", None),
            P(("row", "col"), "dp", None),
            P(("row", "col"), "dp", None),
        ),
        check_vma=False,
    )
```

```python
import functools
import math

import jax
import jax.numpy as jnp
from jax import lax
from jax.experimental import pallas as pl
from jax.experimental.pallas import tpu as pltpu
from jax.sharding import PartitionSpec as P

MESH = pl.DeviceIdType.MESH
GAMMA = 1.7015043497085571
ALPHA = 0.2
EPS = 1e-06
G = 128
FAN = 9 * G
ROOT = math.sqrt(FAN)
NY, NZ, NX = 4, 2, 4
MEMBERS = NZ * NX
H, W = 8, 64
PIX = H * W
BF = jnp.bfloat16
F32 = jnp.float32
CUBE = 0.044715
SLOPE = math.sqrt(2 / math.pi)


def gelu_pair(x):
    square = x * x
    t = jnp.tanh(SLOPE * x * (1.0 + CUBE * square))
    half = (0.5 * GAMMA) * (1.0 + t)
    value = half * x
    slope = half + (0.5 * GAMMA * SLOPE) * x * (1.0 - t * t) * (1.0 + (3.0 * CUBE) * square)
    return value, slope


def column(gain):
    n = gain.shape[1]
    eye = lax.broadcasted_iota(jnp.int32, (n, n), 0) == lax.broadcasted_iota(jnp.int32, (n, n), 1)
    return jnp.sum(jnp.where(eye, jnp.broadcast_to(gain, (n, n)), 0.0), axis=1, keepdims=True)


def centre(kernel):
    c = kernel - jnp.mean(kernel, axis=1, keepdims=True)
    r = lax.rsqrt(jnp.mean(c * c, axis=1, keepdims=True) + EPS)
    return c, r


def body(
    feat, cot, k1_hbm, k2_hbm, g1_hbm, g2_hbm,
    out, igrad, kg1, kg2,
    k1, k2, g1, g2, kout1, kout2, p_sem, xin, cin, obuf, ibuf, shard, wall, wf, wa, apad, hpad, gpad, zpad, slope_x, slope_z,
    acc, gsend, grecv, zsend, zrecv,
    in_send, in_recv, w_send, w_recv, o_send, o_recv, g_send, g_recv,
):
    dp, row, col = lax.axis_index("dp"), lax.axis_index("row"), lax.axis_index("col")
    y, m = dp // MEMBERS, dp % MEMBERS
    spot = row * 2 + col
    seat = y * 4 + spot
    group = spot * NY + y

    zh, x = m // NX, m % NX

    def peer(step, p):
        py = lax.rem(y + step, NY)
        return (py * MEMBERS + m, p // 2, p % 2), py

    def along(j):
        return (y * MEMBERS + zh * NX + lax.rem(x + j, NX), row, col)

    other = (1 - zh) * NX + x
    partner = (y * MEMBERS + other, row, col)

    params = [
        pltpu.make_async_copy(s, d, p_sem.at[i])
        for i, (s, d) in enumerate(((k1_hbm, k1), (k2_hbm, k2), (g1_hbm, g1), (g2_hbm, g2)))
    ]
    for copy in params:
        copy.start()
    barrier = pltpu.get_barrier_semaphore()

    @pl.loop(1, 16)
    def _(k):
        step, p = k // 4, lax.rem(spot + k % 4, 4)
        pl.semaphore_signal(barrier, inc=1, device_id=peer(step, p)[0], device_id_type=MESH)

    for j in range(1, NX):
        pl.semaphore_signal(barrier, inc=1, device_id=along(j), device_id_type=MESH)
    pl.semaphore_signal(barrier, inc=1, device_id=partner, device_id_type=MESH)

    for copy in params:
        copy.wait()
    gains = (column(g1[...]), column(g2[...]))
    for idx, k in enumerate((k1, k2)):
        c, r = centre(k[0])
        shard[idx] = (gains[idx] * c * r / ROOT).astype(BF)
    zero = jnp.zeros((W, G), BF)
    for pad in (apad, hpad, gpad, zpad):
        pad[0:W] = zero
        pad[W + PIX : 2 * W + PIX] = zero
    acc[...] = jnp.zeros_like(acc)

    pl.semaphore_wait(barrier, 15 + NX)

    def in_copy(which, step, p):
        src, dst = ((feat, xin), (cot, cin))[which]
        dev, py = peer(step, p)
        lane = pl.multiple_of((p * NY + py) * G, G)
        s = src.at[0, :, :, pl.ds(lane, G)]
        d = dst.at[y, pl.ds(row * 4, 4), pl.ds(pl.multiple_of(col * 32, 32), 32), :]
        return s, d, dev

    def in_remote(which, step, p):
        s, d, dev = in_copy(which, step, p)
        return pltpu.make_async_remote_copy(
            src_ref=s, dst_ref=d, send_sem=in_send.at[which, step, p],
            recv_sem=in_recv.at[which, y], device_id=dev, device_id_type=MESH,
        )

    def own_copy(which):
        s, d, _ = in_copy(which, 0, spot)
        return pltpu.make_async_copy(s, d, in_recv.at[which, y])

    def rows(member):
        return wall.at[:, pl.ds(pl.multiple_of(member * 16, 16), 16), :]

    def w_send_to(src, member, dev, slot, recv):
        return pltpu.make_async_remote_copy(
            src_ref=src, dst_ref=rows(member), send_sem=w_send.at[slot], recv_sem=w_recv.at[recv],
            device_id=dev, device_id_type=MESH,
        )

    w_across = w_send_to(shard, m, partner, 0, 0)
    w_first = [w_send_to(shard, m, along(j), j, 1) for j in range(1, NX)]
    w_second = [w_send_to(rows(other), other, along(j), NX - 1 + j, 1) for j in range(1, NX)]
    w_own = pltpu.make_async_copy(shard, rows(m), w_recv.at[2])
    w_across.start()
    for copy in w_first:
        copy.start()
    w_own.start()
    own_copy(0).start()
    own_copy(1).start()

    @pl.loop(1, 4)
    def _(k):
        p = lax.rem(spot + k, 4)
        in_remote(0, 0, p).start()
        in_remote(1, 0, p).start()

    for step in (3, 1, 2):
        @pl.loop(0, 4)
        def _(p):
            in_remote(0, step, p).start()
            in_remote(1, step, p).start()

    w_across.wait_recv()
    for copy in w_second:
        copy.start()
    w_own.wait()
    gathered = wall.at[:, 0 : 2 * (NX - 1) * 16, :]
    pltpu.make_async_copy(gathered, gathered, w_recv.at[1]).wait()
    for idx in range(2):
        for dy in range(3):
            wa[idx, dy * G : (dy + 1) * G, :] = wall[idx, :, 3 * G * dy : 3 * G * (dy + 1)]
            for dx in range(3):
                wf[idx, dx * G : (dx + 1) * G, dy * G : (dy + 1) * G] = wall[
                    idx, :, (3 * dy + dx) * G : (3 * dy + dx + 1) * G
                ]

    where = lax.broadcasted_iota(jnp.int32, (PIX, G), 0) % W
    first, last = where == 0, where == W - 1

    def later(v):
        return jnp.where(first, 0.0, pltpu.roll(v, 1, 0))

    def sooner(v):
        return jnp.where(last, 0.0, pltpu.roll(v, PIX - 1, 0))

    def stack(pad, order):
        return jnp.concatenate([pad[d * W : d * W + PIX] for d in order], axis=1)

    def forward(pad, idx):
        p = lax.dot_general(
            stack(pad, (0, 1, 2)), wf[idx], (((1,), (1,)), ((), ())), preferred_element_type=F32
        )
        return later(p[:, :G]) + p[:, G : 2 * G] + sooner(p[:, 2 * G :])

    def adjoint(pad, idx):
        p = jnp.dot(stack(pad, (2, 1, 0)), wa[idx], preferred_element_type=F32)
        return sooner(p[:, :G]) + p[:, G : 2 * G] + later(p[:, 2 * G :])

    def terms(v, pad, idx):
        g = jnp.concatenate([sooner(v).astype(BF), v.astype(BF), later(v).astype(BF)], axis=1)
        acc[idx] += lax.dot_general(
            g, stack(pad, (0, 1, 2)), (((0,), (0,)), ((), ())), preferred_element_type=F32
        )

    def out_remote(which, n, p):
        src, dst = ((obuf, out), (ibuf, igrad))[which]
        prow, pcol = p // 2, p % 2
        s = src.at[n, pl.ds(prow * 4, 4), pl.ds(pl.multiple_of(pcol * 32, 32), 32), :]
        d = dst.at[0, :, :, pl.ds(pl.multiple_of(group * G, G), G)]
        return s, d, (n * MEMBERS + m, prow, pcol), n * 4 + p

    def out_start(which, n):
        @pl.loop(0, 4)
        def _(p):
            s, d, dev, slot = out_remote(which, n, p)
            mine = slot == seat

            @pl.when(mine)
            def _():
                pltpu.make_async_copy(s, d, o_recv.at[which]).start()

            @pl.when(jnp.logical_not(mine))
            def _():
                pltpu.make_async_remote_copy(
                    src_ref=s, dst_ref=d, send_sem=o_send.at[which, slot],
                    recv_sem=o_recv.at[which], device_id=dev, device_id_type=MESH,
                ).start()

    def g_along(step):
        return pltpu.make_async_remote_copy(
            src_ref=gsend.at[lax.rem(x + step, NX)], dst_ref=grecv.at[x], send_sem=g_send.at[step],
            recv_sem=g_recv.at[0], device_id=along(step), device_id_type=MESH,
        )

    g_across = pltpu.make_async_remote_copy(
        src_ref=zsend, dst_ref=zrecv, send_sem=g_send.at[0], recv_sem=g_recv.at[1],
        device_id=partner, device_id_type=MESH,
    )

    @pl.loop(0, NY)
    def _(j):
        n = lax.rem(y + j + (j // 2) * (5 - 2 * j), NY)
        pltpu.make_async_copy(xin.at[n], xin.at[n], in_recv.at[0, n]).wait()
        x = xin[n].reshape(PIX, G).astype(F32)
        value, slope = gelu_pair(x)
        slope_x[...] = slope
        apad[W : W + PIX] = value.astype(BF)
        z = forward(apad, 0).astype(BF).astype(F32)
        value, slope = gelu_pair(z)
        slope_z[...] = slope
        hpad[W : W + PIX] = value.astype(BF)
        pltpu.make_async_copy(cin.at[n], cin.at[n], in_recv.at[1, n]).wait()
        upper = (ALPHA * cin[n].reshape(PIX, G).astype(F32)).astype(BF)
        gpad[W : W + PIX] = upper
        lower = (adjoint(gpad, 1) * slope_z[...]).astype(BF)
        zpad[W : W + PIX] = lower
        terms(gpad[W : W + PIX].astype(F32), hpad, 1)
        terms(zpad[W : W + PIX].astype(F32), apad, 0)

        @pl.when(j == NY - 1)
        def _():
            for member in range(MEMBERS):
                for idx in range(2):
                    for tap in range(9):
                        dy, dx = tap // 3, tap % 3
                        gsend[member % NX, member // NX, idx, :, tap * G : (tap + 1) * G] = acc[
                            idx, dx * G + member * 16 : dx * G + member * 16 + 16, dy * G : (dy + 1) * G
                        ].astype(BF)

        res = xin[n].reshape(PIX, G).astype(F32) + ALPHA * forward(hpad, 1)
        obuf[n] = res.astype(BF).reshape(H, W, G)

        @pl.when(j == NY - 1)
        def _():
            for step in range(1, NX):
                g_along(step).start()

        back = adjoint(zpad, 0)
        out_start(0, n)
        ig = cin[n].reshape(PIX, G).astype(F32) + slope_x[...] * back
        ibuf[n] = ig.astype(BF).reshape(H, W, G)
        out_start(1, n)

    for step in range(4):
        @pl.loop(0, 4)
        def _(p):
            @pl.when(jnp.logical_or(p != spot, step != 0))
            def _():
                in_remote(0, step, p).wait_send()
                in_remote(1, step, p).wait_send()

    for copy in [w_across] + w_first + w_second:
        copy.wait_send()
    arrived = grecv.at[0 : NX - 1]
    pltpu.make_async_copy(arrived, arrived, g_recv.at[0]).wait()

    def summed(half, idx):
        total = gsend[x, half, idx].astype(F32)
        for step in range(1, NX):
            total = total + grecv[lax.rem(x + step, NX), half, idx].astype(F32)
        return total

    for idx in range(2):
        zsend[idx] = summed(1 - zh, idx).astype(BF)
    mine = [summed(zh, idx) for idx in range(2)]
    g_across.start()
    g_across.wait_recv()
    for idx, (k, kg) in enumerate(((k1, kout1), (k2, kout2))):
        total = mine[idx] + zrecv[idx].astype(F32)
        c, r = centre(k[0])
        scale = gains[idx] * r / ROOT
        d = scale * (total - c * (r * r * jnp.mean(total * c, axis=1, keepdims=True)))
        kg[0] = d - jnp.mean(d, axis=1, keepdims=True)
    finals = [
        pltpu.make_async_copy(s, d, p_sem.at[i]) for i, (s, d) in enumerate(((kout1, kg1), (kout2, kg2)))
    ]
    for copy in finals:
        copy.start()

    g_across.wait_send()
    for step in range(1, NX):
        g_along(step).wait_send()

    for which in range(2):
        @pl.loop(0, 16)
        def _(slot):
            @pl.when(slot != seat)
            def _():
                s, d, dev, _ = out_remote(which, slot // 4, slot % 4)
                pltpu.make_async_remote_copy(
                    src_ref=s, dst_ref=d, send_sem=o_send.at[which, slot],
                    recv_sem=o_recv.at[which], device_id=dev, device_id_type=MESH,
                ).wait_send()

        dst = (out, igrad)[which]
        pltpu.make_async_copy(dst, dst, o_recv.at[which]).wait()
    for copy in finals:
        copy.wait()


def deliver(a, b, c, d, ao, bo, co, do, av, bv, cv, dv, sem_in, sem_out):
    halves = []
    for s, v, t in ((a, av, ao), (b, bv, bo)):
        for h in range(2):
            halves.append((s.at[:, 2 * h : 2 * h + 2], v.at[:, 2 * h : 2 * h + 2], t.at[:, 2 * h : 2 * h + 2]))
    halves += [(c, cv, co), (d, dv, do)]
    ins = [pltpu.make_async_copy(s, v, sem_in.at[i]) for i, (s, v, _) in enumerate(halves)]
    outs = [pltpu.make_async_copy(v, t, sem_out.at[i]) for i, (_, v, t) in enumerate(halves)]
    for copy in ins:
        copy.start()
    for first, second in zip(ins, outs):
        first.wait()
        second.start()
    for copy in outs:
        copy.wait()


def local(features, cotangent, kernel_one, kernel_two, gain_one, gain_two):
    hbm = pl.BlockSpec(memory_space=pltpu.HBM)
    raw = pl.BlockSpec(memory_space=pl.ANY)
    vm = pltpu.VMEM
    dma = pltpu.SemaphoreType.DMA
    shapes = (
        jax.ShapeDtypeStruct(features.shape, BF),
        jax.ShapeDtypeStruct(features.shape, BF),
        jax.ShapeDtypeStruct(kernel_one.shape, F32),
        jax.ShapeDtypeStruct(kernel_two.shape, F32),
    )
    results = pl.pallas_call(
        body,
        out_shape=shapes,
        in_specs=[hbm] * 6,
        out_specs=(raw,) * 4,
        scratch_shapes=[
            vm((1, 16, FAN), F32), vm((1, 16, FAN), F32), vm((1, 16), F32), vm((1, 16), F32),
            vm((1, 16, FAN), F32), vm((1, 16, FAN), F32), dma((4,)),
            vm((NY, H, W, G), BF), vm((NY, H, W, G), BF),
            vm((NY, H, W, G), BF), vm((NY, H, W, G), BF),
            vm((2, 16, FAN), BF), vm((2, G, FAN), BF),
            vm((2, 3 * G, 3 * G), BF), vm((2, 3 * G, 3 * G), BF),
            vm((PIX + 2 * W, G), BF), vm((PIX + 2 * W, G), BF),
            vm((PIX + 2 * W, G), BF), vm((PIX + 2 * W, G), BF),
            vm((PIX, G), F32), vm((PIX, G), F32),
            vm((2, 3 * G, 3 * G), F32),
            vm((NX, NZ, 2, 16, FAN), BF), vm((NX, NZ, 2, 16, FAN), BF),
            vm((2, 16, FAN), BF), vm((2, 16, FAN), BF),
            dma((2, NY, 4)), dma((2, NY)), dma((2 * NX - 1,)), dma((3,)),
            dma((2, 16)), dma((2,)), dma((NX,)), dma((2,)),
        ],
        compiler_params=pltpu.CompilerParams(
            collective_id=0, has_side_effects=True, vmem_limit_bytes=60 << 20
        ),
        name="block",
    )(features, cotangent, kernel_one, kernel_two, gain_one, gain_two)
    return pl.pallas_call(
        deliver,
        out_shape=shapes,
        in_specs=[raw] * 4,
        out_specs=(raw,) * 4,
        scratch_shapes=[vm(s.shape, s.dtype) for s in shapes] + [dma((6,)), dma((6,))],
        name="deliver",
    )(*results)


def solution(mesh):
    return jax.shard_map(
        local,
        mesh=mesh,
        in_specs=(
            P("dp", "row", "col", None),
            P("dp", "row", "col", None),
            P(("row", "col"), "dp", None),
            P(("row", "col"), "dp", None),
            P(("row", "col"), "dp"),
            P(("row", "col"), "dp"),
        ),
        out_specs=(
            P("dp", "row", "col", None),
            P("dp", "row", "col", None),
            P(("row", "col"), "dp", None),
            P(("row", "col"), "dp", None),
        ),
        check_vma=False,
    )
```

```python
import functools
import math

import jax
import jax.numpy as jnp
from jax import lax
from jax.experimental import pallas as pl
from jax.experimental.pallas import tpu as pltpu
from jax.sharding import PartitionSpec as P

MESH = pl.DeviceIdType.MESH
GAMMA = 1.7015043497085571
ALPHA = 0.2
EPS = 1e-06
G = 128
FAN = 9 * G
ROOT = math.sqrt(FAN)
NY, NZ, NX = 4, 2, 4
MEMBERS = NZ * NX
H, W = 8, 64
PIX = H * W
BF = jnp.bfloat16
F32 = jnp.float32
CUBE = 0.044715
SLOPE = math.sqrt(2 / math.pi)


def gelu_pair(x):
    square = x * x
    t = jnp.tanh(SLOPE * x * (1.0 + CUBE * square))
    half = (0.5 * GAMMA) * (1.0 + t)
    value = half * x
    slope = half + (0.5 * GAMMA * SLOPE) * x * (1.0 - t * t) * (1.0 + (3.0 * CUBE) * square)
    return value, slope


def column(gain):
    n = gain.shape[1]
    eye = lax.broadcasted_iota(jnp.int32, (n, n), 0) == lax.broadcasted_iota(jnp.int32, (n, n), 1)
    return jnp.sum(jnp.where(eye, jnp.broadcast_to(gain, (n, n)), 0.0), axis=1, keepdims=True)


def centre(kernel):
    c = kernel - jnp.mean(kernel, axis=1, keepdims=True)
    r = lax.rsqrt(jnp.mean(c * c, axis=1, keepdims=True) + EPS)
    return c, r


def body(
    feat, cot, k1_hbm, k2_hbm, g1_hbm, g2_hbm,
    out, igrad, kg1, kg2,
    k1, k2, g1, g2, kout1, kout2, p_sem, xin, cin, obuf, ibuf, shard, wall, wf, wa, apad, hpad, gpad, zpad, slope_x, slope_z,
    acc, gsend, grecv, zsend, zrecv,
    in_send, in_recv, w_send, w_recv, o_send, o_recv, g_send, g_recv,
):
    dp, row, col = lax.axis_index("dp"), lax.axis_index("row"), lax.axis_index("col")
    y, m = dp // MEMBERS, dp % MEMBERS
    spot = row * 2 + col
    seat = y * 4 + spot
    group = spot * NY + y

    zh, x = m // NX, m % NX

    def peer(step, p):
        py = lax.rem(y + step, NY)
        return (py * MEMBERS + m, p // 2, p % 2), py

    def along(j):
        return (y * MEMBERS + zh * NX + lax.rem(x + j, NX), row, col)

    other = (1 - zh) * NX + x
    partner = (y * MEMBERS + other, row, col)

    params = [
        pltpu.make_async_copy(s, d, p_sem.at[i])
        for i, (s, d) in enumerate(((k1_hbm, k1), (k2_hbm, k2), (g1_hbm, g1), (g2_hbm, g2)))
    ]
    for copy in params:
        copy.start()
    barrier = pltpu.get_barrier_semaphore()

    @pl.loop(1, 16)
    def _(k):
        step, p = k // 4, lax.rem(spot + k % 4, 4)
        pl.semaphore_signal(barrier, inc=1, device_id=peer(step, p)[0], device_id_type=MESH)

    for j in range(1, NX):
        pl.semaphore_signal(barrier, inc=1, device_id=along(j), device_id_type=MESH)
    pl.semaphore_signal(barrier, inc=1, device_id=partner, device_id_type=MESH)

    for copy in params:
        copy.wait()
    gains = (column(g1[...]), column(g2[...]))
    for idx, k in enumerate((k1, k2)):
        c, r = centre(k[0])
        shard[idx] = (gains[idx] * c * r / ROOT).astype(BF)
    zero = jnp.zeros((W, G), BF)
    for pad in [p.at[n] for p in (apad, hpad, gpad, zpad) for n in range(NY)]:
        pad[0:W] = zero
        pad[W + PIX : 2 * W + PIX] = zero
    acc[...] = jnp.zeros_like(acc)

    pl.semaphore_wait(barrier, 15 + NX)

    def in_copy(which, step, p):
        src, dst = ((feat, xin), (cot, cin))[which]
        dev, py = peer(step, p)
        lane = pl.multiple_of((p * NY + py) * G, G)
        s = src.at[0, :, :, pl.ds(lane, G)]
        d = dst.at[y, pl.ds(row * 4, 4), pl.ds(pl.multiple_of(col * 32, 32), 32), :]
        return s, d, dev

    def in_remote(which, step, p):
        s, d, dev = in_copy(which, step, p)
        return pltpu.make_async_remote_copy(
            src_ref=s, dst_ref=d, send_sem=in_send.at[which, step, p],
            recv_sem=in_recv.at[which, y], device_id=dev, device_id_type=MESH,
        )

    def own_copy(which):
        s, d, _ = in_copy(which, 0, spot)
        return pltpu.make_async_copy(s, d, in_recv.at[which, y])

    def rows(member):
        return wall.at[:, pl.ds(pl.multiple_of(member * 16, 16), 16), :]

    def w_send_to(idx, src, member, dev, slot, recv):
        return pltpu.make_async_remote_copy(
            src_ref=src.at[idx], dst_ref=rows(member).at[idx], send_sem=w_send.at[idx, slot],
            recv_sem=w_recv.at[idx, recv], device_id=dev, device_id_type=MESH,
        )

    w_across = [w_send_to(idx, shard, m, partner, 0, 0) for idx in range(2)]
    w_first = [[w_send_to(idx, shard, m, along(j), j, 1) for j in range(1, NX)] for idx in range(2)]
    w_second = [
        [w_send_to(idx, rows(other), other, along(j), NX - 1 + j, 1) for j in range(1, NX)]
        for idx in range(2)
    ]
    w_own = pltpu.make_async_copy(shard, rows(m), w_recv.at[0, 2])
    for copy in w_across + w_first[0] + w_first[1] + [w_own]:
        copy.start()
    own_copy(0).start()
    own_copy(1).start()

    def in_start(step, prow):
        for which in range(2):
            @pl.loop(0, 2)
            def _(pcol):
                in_remote(which, step, prow * 2 + pcol).start()

    def in_wait(which, n):
        src = (xin, cin)[which]
        pltpu.make_async_copy(src.at[n], src.at[n], in_recv.at[which, n]).wait()

    for which in range(2):
        in_remote(which, 0, row * 2 + 1 - col).start()
    in_start(0, 1 - row)
    in_start(3, row)
    in_start(1, row)
    in_start(2, row)
    w_across[0].wait_recv()
    for copy in w_second[0]:
        copy.start()
    in_start(3, 1 - row)
    in_start(1, 1 - row)
    in_start(2, 1 - row)
    w_across[1].wait_recv()
    for copy in w_second[1]:
        copy.start()
    w_own.wait()

    def w_ready(idx):
        gathered = wall.at[idx, 0 : 2 * (NX - 1) * 16, :]
        pltpu.make_async_copy(gathered, gathered, w_recv.at[idx, 1]).wait()
        for dy in range(3):
            wa[idx, dy * G : (dy + 1) * G, :] = wall[idx, :, 3 * G * dy : 3 * G * (dy + 1)]
            for dx in range(3):
                wf[idx, dx * G : (dx + 1) * G, dy * G : (dy + 1) * G] = wall[
                    idx, :, (3 * dy + dx) * G : (3 * dy + dx + 1) * G
                ]

    where = lax.broadcasted_iota(jnp.int32, (PIX, G), 0) % W
    first, last = where == 0, where == W - 1

    def later(v):
        return jnp.where(first, 0.0, pltpu.roll(v, 1, 0))

    def sooner(v):
        return jnp.where(last, 0.0, pltpu.roll(v, PIX - 1, 0))

    def stack(pad, order):
        return jnp.concatenate([pad[d * W : d * W + PIX] for d in order], axis=1)

    def forward(pad, idx):
        p = lax.dot_general(
            stack(pad, (0, 1, 2)), wf[idx], (((1,), (1,)), ((), ())), preferred_element_type=F32
        )
        return later(p[:, :G]) + p[:, G : 2 * G] + sooner(p[:, 2 * G :])

    def adjoint(pad, idx):
        p = jnp.dot(stack(pad, (2, 1, 0)), wa[idx], preferred_element_type=F32)
        return sooner(p[:, :G]) + p[:, G : 2 * G] + later(p[:, 2 * G :])

    def terms(v, pad, idx):
        g = jnp.concatenate([sooner(v).astype(BF), v.astype(BF), later(v).astype(BF)], axis=1)
        acc[idx] += lax.dot_general(
            g, stack(pad, (0, 1, 2)), (((0,), (0,)), ((), ())), preferred_element_type=F32
        )

    def out_remote(which, n, p):
        src, dst = ((obuf, out), (ibuf, igrad))[which]
        prow, pcol = p // 2, p % 2
        s = src.at[n, pl.ds(prow * 4, 4), pl.ds(pl.multiple_of(pcol * 32, 32), 32), :]
        d = dst.at[0, :, :, pl.ds(pl.multiple_of(group * G, G), G)]
        return s, d, (n * MEMBERS + m, prow, pcol), n * 4 + p

    def out_start(which, n):
        @pl.loop(0, 4)
        def _(p):
            s, d, dev, slot = out_remote(which, n, p)
            mine = slot == seat

            @pl.when(mine)
            def _():
                pltpu.make_async_copy(s, d, o_recv.at[which]).start()

            @pl.when(jnp.logical_not(mine))
            def _():
                pltpu.make_async_remote_copy(
                    src_ref=s, dst_ref=d, send_sem=o_send.at[which, slot],
                    recv_sem=o_recv.at[which], device_id=dev, device_id_type=MESH,
                ).start()

    def g_along(idx, step):
        return pltpu.make_async_remote_copy(
            src_ref=gsend.at[idx, lax.rem(x + step, NX)], dst_ref=grecv.at[idx, x],
            send_sem=g_send.at[idx, step], recv_sem=g_recv.at[idx, 0],
            device_id=along(step), device_id_type=MESH,
        )

    g_across = [
        pltpu.make_async_remote_copy(
            src_ref=zsend.at[idx], dst_ref=zrecv.at[idx], send_sem=g_send.at[idx, 0],
            recv_sem=g_recv.at[idx, 1], device_id=partner, device_id_type=MESH,
        )
        for idx in range(2)
    ]

    def pack(idx):
        for member in range(MEMBERS):
            for tap in range(9):
                dy, dx = tap // 3, tap % 3
                gsend[idx, member % NX, member // NX, :, tap * G : (tap + 1) * G] = acc[
                    idx, dx * G + member * 16 : dx * G + member * 16 + 16, dy * G : (dy + 1) * G
                ].astype(BF)

    def order(j):
        return lax.rem(y + (0, 1, 3, 2)[j], NY)

    def results(n):
        res = xin[n].reshape(PIX, G).astype(F32) + ALPHA * forward(hpad.at[n], 1)
        obuf[n] = res.astype(BF).reshape(H, W, G)
        back = adjoint(zpad.at[n], 0)
        out_start(0, n)
        ig = cin[n].reshape(PIX, G).astype(F32) + slope_x[n] * back
        ibuf[n] = ig.astype(BF).reshape(H, W, G)
        out_start(1, n)

    def hidden(n):
        value, slope = gelu_pair(xin[n].reshape(PIX, G).astype(F32))
        slope_x[n] = slope
        apad[n, W : W + PIX] = value.astype(BF)
        z = forward(apad.at[n], 0).astype(BF).astype(F32)
        value, slope = gelu_pair(z)
        slope_z[n] = slope
        hpad[n, W : W + PIX] = value.astype(BF)
        gpad[n, W : W + PIX] = (ALPHA * cin[n].reshape(PIX, G).astype(F32)).astype(BF)
        terms(gpad[n, W : W + PIX].astype(F32), hpad.at[n], 1)

    def lower(n):
        zpad[n, W : W + PIX] = (adjoint(gpad.at[n], 1) * slope_z[n]).astype(BF)

    def lower_terms(n):
        terms(zpad[n, W : W + PIX].astype(F32), apad.at[n], 0)

    images = [order(j) for j in range(NY)]
    n0, n1, n2, n3 = images
    w_ready(0)
    in_wait(0, n0)
    in_wait(1, n0)
    hidden(n0)
    w_ready(1)
    lower(n0)
    lower_terms(n0)
    results(n0)
    in_wait(0, n1)
    in_wait(1, n1)
    hidden(n1)
    lower(n1)
    lower_terms(n1)
    results(n1)
    in_wait(0, n2)
    in_wait(1, n2)
    hidden(n2)
    lower(n2)
    lower_terms(n2)
    results(n2)
    in_wait(0, n3)
    in_wait(1, n3)
    hidden(n3)
    pack(1)
    lower(n3)
    for step in range(1, NX):
        g_along(1, step).start()
    lower_terms(n3)
    pack(0)
    for step in range(1, NX):
        g_along(0, step).start()
    for n in (n3,):
        results(n)

    for step in range(4):
        @pl.loop(0, 4)
        def _(p):
            @pl.when(jnp.logical_or(p != spot, step != 0))
            def _():
                in_remote(0, step, p).wait_send()
                in_remote(1, step, p).wait_send()

    for copy in w_across + w_first[0] + w_first[1] + w_second[0] + w_second[1]:
        copy.wait_send()
    def summed(half, idx):
        total = gsend[idx, x, half].astype(F32)
        for step in range(1, NX):
            total = total + grecv[idx, lax.rem(x + step, NX), half].astype(F32)
        return total

    mine = {}
    for idx in (1, 0):
        arrived = grecv.at[idx, 0 : NX - 1]
        pltpu.make_async_copy(arrived, arrived, g_recv.at[idx, 0]).wait()
        zsend[idx] = summed(1 - zh, idx).astype(BF)
        mine[idx] = summed(zh, idx)
        g_across[idx].start()
    for idx, k, kg in ((1, k2, kout2), (0, k1, kout1)):
        g_across[idx].wait_recv()
        total = mine[idx] + zrecv[idx].astype(F32)
        c, r = centre(k[0])
        scale = gains[idx] * r / ROOT
        d = scale * (total - c * (r * r * jnp.mean(total * c, axis=1, keepdims=True)))
        kg[0] = d - jnp.mean(d, axis=1, keepdims=True)
    finals = [
        pltpu.make_async_copy(s, d, p_sem.at[i]) for i, (s, d) in enumerate(((kout1, kg1), (kout2, kg2)))
    ]
    for copy in finals:
        copy.start()

    for idx in range(2):
        g_across[idx].wait_send()
        for step in range(1, NX):
            g_along(idx, step).wait_send()

    for which in range(2):
        @pl.loop(0, 16)
        def _(slot):
            @pl.when(slot != seat)
            def _():
                s, d, dev, _ = out_remote(which, slot // 4, slot % 4)
                pltpu.make_async_remote_copy(
                    src_ref=s, dst_ref=d, send_sem=o_send.at[which, slot],
                    recv_sem=o_recv.at[which], device_id=dev, device_id_type=MESH,
                ).wait_send()

        dst = (out, igrad)[which]
        pltpu.make_async_copy(dst, dst, o_recv.at[which]).wait()
    for copy in finals:
        copy.wait()


def deliver(a, b, c, d, ao, bo, co, do, av, bv, cv, dv, sem_in, sem_out):
    halves = []
    for s, v, t in ((a, av, ao), (b, bv, bo)):
        for h in range(2):
            halves.append((s.at[:, 2 * h : 2 * h + 2], v.at[:, 2 * h : 2 * h + 2], t.at[:, 2 * h : 2 * h + 2]))
    halves += [(c, cv, co), (d, dv, do)]
    ins = [pltpu.make_async_copy(s, v, sem_in.at[i]) for i, (s, v, _) in enumerate(halves)]
    outs = [pltpu.make_async_copy(v, t, sem_out.at[i]) for i, (_, v, t) in enumerate(halves)]
    for copy in ins:
        copy.start()
    for first, second in zip(ins, outs):
        first.wait()
        second.start()
    for copy in outs:
        copy.wait()


def local(features, cotangent, kernel_one, kernel_two, gain_one, gain_two):
    hbm = pl.BlockSpec(memory_space=pltpu.HBM)
    raw = pl.BlockSpec(memory_space=pl.ANY)
    vm = pltpu.VMEM
    dma = pltpu.SemaphoreType.DMA
    shapes = (
        jax.ShapeDtypeStruct(features.shape, BF),
        jax.ShapeDtypeStruct(features.shape, BF),
        jax.ShapeDtypeStruct(kernel_one.shape, F32),
        jax.ShapeDtypeStruct(kernel_two.shape, F32),
    )
    results = pl.pallas_call(
        body,
        out_shape=shapes,
        in_specs=[hbm] * 6,
        out_specs=(raw,) * 4,
        scratch_shapes=[
            vm((1, 16, FAN), F32), vm((1, 16, FAN), F32), vm((1, 16), F32), vm((1, 16), F32),
            vm((1, 16, FAN), F32), vm((1, 16, FAN), F32), dma((4,)),
            vm((NY, H, W, G), BF), vm((NY, H, W, G), BF),
            vm((NY, H, W, G), BF), vm((NY, H, W, G), BF),
            vm((2, 16, FAN), BF), vm((2, G, FAN), BF),
            vm((2, 3 * G, 3 * G), BF), vm((2, 3 * G, 3 * G), BF),
            vm((NY, PIX + 2 * W, G), BF), vm((NY, PIX + 2 * W, G), BF),
            vm((NY, PIX + 2 * W, G), BF), vm((NY, PIX + 2 * W, G), BF),
            vm((NY, PIX, G), F32), vm((NY, PIX, G), F32),
            vm((2, 3 * G, 3 * G), F32),
            vm((2, NX, NZ, 16, FAN), BF), vm((2, NX, NZ, 16, FAN), BF),
            vm((2, 16, FAN), BF), vm((2, 16, FAN), BF),
            dma((2, NY, 4)), dma((2, NY)), dma((2, 2 * NX - 1)), dma((2, 3)),
            dma((2, 16)), dma((2,)), dma((2, NX)), dma((2, 2)),
        ],
        compiler_params=pltpu.CompilerParams(
            collective_id=0, has_side_effects=True, vmem_limit_bytes=60 << 20
        ),
        name="block",
    )(features, cotangent, kernel_one, kernel_two, gain_one, gain_two)
    return pl.pallas_call(
        deliver,
        out_shape=shapes,
        in_specs=[raw] * 4,
        out_specs=(raw,) * 4,
        scratch_shapes=[vm(s.shape, s.dtype) for s in shapes] + [dma((6,)), dma((6,))],
        name="deliver",
    )(*results)


def solution(mesh):
    return jax.shard_map(
        local,
        mesh=mesh,
        in_specs=(
            P("dp", "row", "col", None),
            P("dp", "row", "col", None),
            P(("row", "col"), "dp", None),
            P(("row", "col"), "dp", None),
            P(("row", "col"), "dp"),
            P(("row", "col"), "dp"),
        ),
        out_specs=(
            P("dp", "row", "col", None),
            P("dp", "row", "col", None),
            P(("row", "col"), "dp", None),
            P(("row", "col"), "dp", None),
        ),
        check_vma=False,
    )
```

```python
import functools
import math

import jax
import jax.numpy as jnp
from jax import lax
from jax.experimental import pallas as pl
from jax.experimental.pallas import tpu as pltpu
from jax.sharding import PartitionSpec as P

MESH = pl.DeviceIdType.MESH
GAMMA = 1.7015043497085571
ALPHA = 0.2
EPS = 1e-06
G = 128
FAN = 9 * G
ROOT = math.sqrt(FAN)
NY, NZ, NX = 4, 2, 4
MEMBERS = NZ * NX
H, W = 8, 64
PIX = H * W
BF = jnp.bfloat16
F32 = jnp.float32
CUBE = 0.044715
SLOPE = math.sqrt(2 / math.pi)


def gelu_pair(x):
    square = x * x
    t = jnp.tanh(SLOPE * x * (1.0 + CUBE * square))
    half = (0.5 * GAMMA) * (1.0 + t)
    value = half * x
    slope = half + (0.5 * GAMMA * SLOPE) * x * (1.0 - t * t) * (1.0 + (3.0 * CUBE) * square)
    return value, slope


def column(gain):
    n = gain.shape[1]
    eye = lax.broadcasted_iota(jnp.int32, (n, n), 0) == lax.broadcasted_iota(jnp.int32, (n, n), 1)
    return jnp.sum(jnp.where(eye, jnp.broadcast_to(gain, (n, n)), 0.0), axis=1, keepdims=True)


def centre(kernel):
    c = kernel - jnp.mean(kernel, axis=1, keepdims=True)
    r = lax.rsqrt(jnp.mean(c * c, axis=1, keepdims=True) + EPS)
    return c, r


def body(
    feat, cot, k1_hbm, k2_hbm, g1_hbm, g2_hbm,
    out, igrad, kg1, kg2,
    k1, k2, g1, g2, kout1, kout2, cent, p_sem, xin, cin, obuf, ibuf, shard, wall, wf, wa, apad, hpad, gpad, zpad, slope_x, slope_z,
    acc, gsend, grecv, zsend, zrecv,
    in_send, in_recv, w_send, w_recv, o_send, o_recv, g_send, g_recv,
):
    dp, row, col = lax.axis_index("dp"), lax.axis_index("row"), lax.axis_index("col")
    y, m = dp // MEMBERS, dp % MEMBERS
    spot = row * 2 + col
    seat = y * 4 + spot
    group = spot * NY + y

    zh, x = m // NX, m % NX

    def peer(step, p):
        py = lax.rem(y + step, NY)
        return (py * MEMBERS + m, p // 2, p % 2), py

    def along(j):
        return (y * MEMBERS + zh * NX + lax.rem(x + j, NX), row, col)

    other = (1 - zh) * NX + x
    partner = (y * MEMBERS + other, row, col)

    params = [
        pltpu.make_async_copy(s, d, p_sem.at[i])
        for i, (s, d) in enumerate(((k1_hbm, k1), (k2_hbm, k2), (g1_hbm, g1), (g2_hbm, g2)))
    ]
    for copy in params:
        copy.start()
    barrier = pltpu.get_barrier_semaphore()

    @pl.loop(1, 16)
    def _(k):
        step, p = k // 4, lax.rem(spot + k % 4, 4)
        pl.semaphore_signal(barrier, inc=1, device_id=peer(step, p)[0], device_id_type=MESH)

    for j in range(1, NX):
        pl.semaphore_signal(barrier, inc=1, device_id=along(j), device_id_type=MESH)
    pl.semaphore_signal(barrier, inc=1, device_id=partner, device_id_type=MESH)

    for copy in params:
        copy.wait()
    gains = (column(g1[...]), column(g2[...]))
    inverse = []
    for idx, k in enumerate((k1, k2)):
        c, r = centre(k[0])
        inverse.append(r)
        cent[idx] = c
        shard[idx] = (gains[idx] * c * r / ROOT).astype(BF)
    zero = jnp.zeros((W, G), BF)
    for pad in [p.at[n] for p in (apad, hpad, gpad, zpad) for n in range(NY)]:
        pad[0:W] = zero
        pad[W + PIX : 2 * W + PIX] = zero
    acc[...] = jnp.zeros_like(acc)
    empty = jnp.zeros((G, G), BF)
    for idx in range(2):
        for dx in range(3):
            for s in range(2):
                at, gap = (2 * dx + s) * G, (3 - 3 * s) * G
                wf[idx, at : at + G, gap : gap + G] = empty
                wa[idx, gap : gap + G, at : at + G] = empty

    pl.semaphore_wait(barrier, 15 + NX)

    def in_copy(which, step, p):
        src, dst = ((feat, xin), (cot, cin))[which]
        dev, py = peer(step, p)
        lane = pl.multiple_of((p * NY + py) * G, G)
        s = src.at[0, :, :, pl.ds(lane, G)]
        d = dst.at[y, pl.ds(row * 4, 4), pl.ds(pl.multiple_of(col * 32, 32), 32), :]
        return s, d, dev

    def in_remote(which, step, p):
        s, d, dev = in_copy(which, step, p)
        return pltpu.make_async_remote_copy(
            src_ref=s, dst_ref=d, send_sem=in_send.at[which, step, p],
            recv_sem=in_recv.at[which, y], device_id=dev, device_id_type=MESH,
        )

    def own_copy(which):
        s, d, _ = in_copy(which, 0, spot)
        return pltpu.make_async_copy(s, d, in_recv.at[which, y])

    def rows(member):
        return wall.at[:, pl.ds(pl.multiple_of(member * 16, 16), 16), :]

    def w_send_to(idx, src, member, dev, slot, recv):
        return pltpu.make_async_remote_copy(
            src_ref=src.at[idx], dst_ref=rows(member).at[idx], send_sem=w_send.at[idx, slot],
            recv_sem=w_recv.at[idx, recv], device_id=dev, device_id_type=MESH,
        )

    w_across = [w_send_to(idx, shard, m, partner, 0, 0) for idx in range(2)]
    w_first = [[w_send_to(idx, shard, m, along(j), j, 1) for j in range(1, NX)] for idx in range(2)]
    w_second = [
        [w_send_to(idx, rows(other), other, along(j), NX - 1 + j, 1) for j in range(1, NX)]
        for idx in range(2)
    ]
    w_own = pltpu.make_async_copy(shard, rows(m), w_recv.at[0, 2])
    for copy in w_across + w_first[0] + w_first[1] + [w_own]:
        copy.start()
    own_copy(0).start()
    own_copy(1).start()

    def in_start(step, prow):
        for pcol in range(2):
            for which in range(2):
                in_remote(which, step, prow * 2 + pcol).start()

    def in_wait(which, n):
        src = (xin, cin)[which]
        pltpu.make_async_copy(src.at[n], src.at[n], in_recv.at[which, n]).wait()

    for which in range(2):
        in_remote(which, 0, row * 2 + 1 - col).start()
    in_start(0, 1 - row)
    in_start(3, row)
    in_start(1, row)
    in_start(2, row)
    w_across[0].wait_recv()
    for copy in w_second[0]:
        copy.start()
    in_start(3, 1 - row)
    in_start(1, 1 - row)
    in_start(2, 1 - row)
    w_across[1].wait_recv()
    for copy in w_second[1]:
        copy.start()
    w_own.wait()

    def w_ready(idx):
        gathered = wall.at[idx, 0 : 2 * (NX - 1) * 16, :]
        pltpu.make_async_copy(gathered, gathered, w_recv.at[idx, 1]).wait()
        for dx in range(3):
            for s in range(2):
                at = (2 * dx + s) * G
                for dy in range(3):
                    block = wall[idx, :, (3 * dy + dx) * G : (3 * dy + dx + 1) * G]
                    wf[idx, at : at + G, (dy + s) * G : (dy + s + 1) * G] = block
                    wa[idx, (s + 2 - dy) * G : (s + 3 - dy) * G, at : at + G] = block

    where = lax.broadcasted_iota(jnp.int32, (PIX, G), 0) % W
    left, right = where == 0, where == W - 1

    def later(v):
        return jnp.where(left[: v.shape[0]], 0.0, pltpu.roll(v, 1, 0))

    def sooner(v):
        return jnp.where(right[: v.shape[0]], 0.0, pltpu.roll(v, v.shape[0] - 1, 0))

    def stack(pad, order):
        return jnp.concatenate([pad[d * W : d * W + PIX] for d in order], axis=1)

    def pairs(pad):
        return jnp.concatenate(
            [
                jnp.concatenate([pad[(2 * t + r) * W : (2 * t + r + 1) * W] for t in range(H // 2)], axis=0)
                for r in range(4)
            ],
            axis=1,
        )

    def weave(p, before, after):
        rows = []
        for s in range(2):
            part = [p[:, (2 * dx + s) * G : (2 * dx + s + 1) * G] for dx in range(3)]
            rows.append(before(part[0]) + part[1] + after(part[2]))
        return jnp.concatenate(
            [rows[s][t * W : (t + 1) * W] for t in range(H // 2) for s in range(2)], axis=0
        )

    def forward(pad, idx):
        p = lax.dot_general(
            pairs(pad), wf[idx], (((1,), (1,)), ((), ())), preferred_element_type=F32
        )
        return weave(p, later, sooner)

    def adjoint(pad, idx):
        p = jnp.dot(pairs(pad), wa[idx], preferred_element_type=F32)
        return weave(p, sooner, later)

    def terms(v, pad, idx):
        g = jnp.concatenate([sooner(v).astype(BF), v.astype(BF), later(v).astype(BF)], axis=1)
        acc[idx] += lax.dot_general(
            g, stack(pad, (0, 1, 2)), (((0,), (0,)), ((), ())), preferred_element_type=F32
        )

    def out_copy(which, n, p):
        src, dst = ((obuf, out), (ibuf, igrad))[which]
        s = src.at[n, pl.ds(p // 2 * 4, 4), pl.ds(pl.multiple_of(p % 2 * 32, 32), 32), :]
        d = dst.at[0, :, :, pl.ds(pl.multiple_of(group * G, G), G)]
        return s, d

    def out_remote(which, n, p):
        s, d = out_copy(which, n, p)
        return pltpu.make_async_remote_copy(
            src_ref=s, dst_ref=d, send_sem=o_send.at[which, n, p], recv_sem=o_recv.at[which],
            device_id=(n * MEMBERS + m, p // 2, p % 2), device_id_type=MESH,
        )

    def out_list(which, n, own):
        return [out_remote(which, n, lax.rem(spot + k, 4)) for k in range(1 if own else 0, 4)]

    def out_start(which, n, own):
        for copy in out_list(which, n, own):
            copy.start()
        if own:
            s, d = out_copy(which, n, spot)
            pltpu.make_async_copy(s, d, o_recv.at[which]).start()

    def g_along(idx, step):
        return pltpu.make_async_remote_copy(
            src_ref=gsend.at[idx, lax.rem(x + step, NX)], dst_ref=grecv.at[idx, x],
            send_sem=g_send.at[idx, step], recv_sem=g_recv.at[idx, 0],
            device_id=along(step), device_id_type=MESH,
        )

    g_across = [
        pltpu.make_async_remote_copy(
            src_ref=zsend.at[idx], dst_ref=zrecv.at[idx], send_sem=g_send.at[idx, 0],
            recv_sem=g_recv.at[idx, 1], device_id=partner, device_id_type=MESH,
        )
        for idx in range(2)
    ]

    def pack(idx):
        for member in range(MEMBERS):
            for tap in range(9):
                dy, dx = tap // 3, tap % 3
                gsend[idx, member % NX, member // NX, :, tap * G : (tap + 1) * G] = acc[
                    idx, dx * G + member * 16 : dx * G + member * 16 + 16, dy * G : (dy + 1) * G
                ].astype(BF)

    def order(j):
        return lax.rem(y + (0, 1, 3, 2)[j], NY)

    def results(n, own=False):
        res = xin[n].reshape(PIX, G).astype(F32) + ALPHA * forward(hpad.at[n], 1)
        obuf[n] = res.astype(BF).reshape(H, W, G)
        back = adjoint(zpad.at[n], 0)
        out_start(0, n, own)
        ig = cin[n].reshape(PIX, G).astype(F32) + slope_x[n] * back
        ibuf[n] = ig.astype(BF).reshape(H, W, G)
        out_start(1, n, own)

    def arrive(n):
        in_wait(0, n)
        in_wait(1, n)

    def first(n):
        value, slope = gelu_pair(xin[n].reshape(PIX, G).astype(F32))
        slope_x[n] = slope
        apad[n, W : W + PIX] = value.astype(BF)
        gpad[n, W : W + PIX] = (ALPHA * cin[n].reshape(PIX, G).astype(F32)).astype(BF)

    def bend(n):
        z = forward(apad.at[n], 0).astype(BF).astype(F32)
        value, slope = gelu_pair(z)
        hpad[n, W : W + PIX] = value.astype(BF)
        return slope

    def lower(n, slope):
        zpad[n, W : W + PIX] = (adjoint(gpad.at[n], 1) * slope).astype(BF)

    def middle(n):
        dh = adjoint(gpad.at[n], 1)
        slope = bend(n)
        zpad[n, W : W + PIX] = (dh * slope).astype(BF)

    def terms_two(n):
        terms(gpad[n, W : W + PIX].astype(F32), hpad.at[n], 1)

    def terms_one(n):
        terms(zpad[n, W : W + PIX].astype(F32), apad.at[n], 0)

    def along_start(idx):
        for step in range(1, NX):
            g_along(idx, step).start()

    images = [order(j) for j in range(NY)]
    n0, n1, n2, n3 = images
    arrive(n0)
    first(n0)
    w_ready(0)
    slope_z[0] = bend(n0)
    terms_two(n0)
    w_ready(1)
    lower(n0, slope_z[0])
    terms_one(n0)
    results(n0, True)
    arrive(n1)
    first(n1)
    middle(n1)
    terms_two(n1)
    terms_one(n1)
    arrive(n2)
    first(n2)
    results(n1)
    middle(n2)
    terms_two(n2)
    terms_one(n2)
    arrive(n3)
    first(n3)
    results(n2)
    middle(n3)
    terms_two(n3)
    pack(1)
    along_start(1)
    terms_one(n3)
    pack(0)
    along_start(0)
    results(n3)

    for step in range(4):
        @pl.loop(0 if step else 1, 4)
        def _(k):
            p = lax.rem(spot + k, 4)
            in_remote(0, step, p).wait_send()
            in_remote(1, step, p).wait_send()

    for copy in w_across + w_first[0] + w_first[1] + w_second[0] + w_second[1]:
        copy.wait_send()
    def summed(half, idx):
        total = gsend[idx, x, half].astype(F32)
        for step in range(1, NX):
            total = total + grecv[idx, lax.rem(x + step, NX), half].astype(F32)
        return total

    mine = {}
    for idx in (1, 0):
        arrived = grecv.at[idx, 0 : NX - 1]
        pltpu.make_async_copy(arrived, arrived, g_recv.at[idx, 0]).wait()
        zsend[idx] = summed(1 - zh, idx).astype(BF)
        mine[idx] = summed(zh, idx)
        g_across[idx].start()
    for n in images:
        for which in range(2):
            for copy in out_list(which, n, n is n0):
                copy.wait_send()
    for idx, kg in ((1, kout2), (0, kout1)):
        g_across[idx].wait_recv()
        total = mine[idx] + zrecv[idx].astype(F32)
        c = cent[idx]
        r = inverse[idx]
        mean_c = jnp.mean(c, axis=1, keepdims=True)
        mean_t = jnp.mean(total, axis=1, keepdims=True)
        pull = r * r * jnp.mean(total * c, axis=1, keepdims=True)
        kg[0] = (gains[idx] * r / ROOT) * ((total - mean_t) - pull * (c - mean_c))
    finals = [
        pltpu.make_async_copy(s, d, p_sem.at[i]) for i, (s, d) in enumerate(((kout1, kg1), (kout2, kg2)))
    ]
    for copy in finals:
        copy.start()

    for idx in range(2):
        g_across[idx].wait_send()
        for step in range(1, NX):
            g_along(idx, step).wait_send()

    for which in range(2):
        dst = (out, igrad)[which]
        pltpu.make_async_copy(dst, dst, o_recv.at[which]).wait()
    for copy in finals:
        copy.wait()


def deliver(a, b, c, d, ao, bo, co, do, sem):
    copies = [
        pltpu.make_async_copy(s, t, sem.at[i])
        for i, (s, t) in enumerate(((a, ao), (b, bo), (c, co), (d, do)))
    ]
    for copy in copies:
        copy.start()
    for copy in copies:
        copy.wait()


def local(features, cotangent, kernel_one, kernel_two, gain_one, gain_two):
    hbm = pl.BlockSpec(memory_space=pltpu.HBM)
    raw = pl.BlockSpec(memory_space=pl.ANY)
    vm = pltpu.VMEM
    dma = pltpu.SemaphoreType.DMA
    shapes = (
        jax.ShapeDtypeStruct(features.shape, BF),
        jax.ShapeDtypeStruct(features.shape, BF),
        jax.ShapeDtypeStruct(kernel_one.shape, F32),
        jax.ShapeDtypeStruct(kernel_two.shape, F32),
    )
    results = pl.pallas_call(
        body,
        out_shape=shapes,
        in_specs=[hbm] * 6,
        out_specs=(raw,) * 4,
        scratch_shapes=[
            vm((1, 16, FAN), F32), vm((1, 16, FAN), F32), vm((1, 16), F32), vm((1, 16), F32),
            vm((1, 16, FAN), F32), vm((1, 16, FAN), F32), vm((2, 16, FAN), F32), dma((4,)),
            vm((NY, H, W, G), BF), vm((NY, H, W, G), BF),
            vm((NY, H, W, G), BF), vm((NY, H, W, G), BF),
            vm((2, 16, FAN), BF), vm((2, G, FAN), BF),
            vm((2, 6 * G, 4 * G), BF), vm((2, 4 * G, 6 * G), BF),
            vm((NY, PIX + 2 * W, G), BF), vm((NY, PIX + 2 * W, G), BF),
            vm((NY, PIX + 2 * W, G), BF), vm((NY, PIX + 2 * W, G), BF),
            vm((NY, PIX, G), F32), vm((1, PIX, G), F32),
            vm((2, 3 * G, 3 * G), F32),
            vm((2, NX, NZ, 16, FAN), BF), vm((2, NX, NZ, 16, FAN), BF),
            vm((2, 16, FAN), BF), vm((2, 16, FAN), BF),
            dma((2, NY, 4)), dma((2, NY)), dma((2, 2 * NX - 1)), dma((2, 3)),
            dma((2, NY, 4)), dma((2,)), dma((2, NX)), dma((2, 2)),
        ],
        compiler_params=pltpu.CompilerParams(
            collective_id=0, has_side_effects=True, vmem_limit_bytes=48 << 20
        ),
        name="block",
    )(*[pltpu.with_memory_space_constraint(v, pltpu.HBM) for v in (features, cotangent, kernel_one, kernel_two, gain_one, gain_two)])
    return pl.pallas_call(
        deliver,
        out_shape=shapes,
        in_specs=[raw] * 4,
        out_specs=(raw,) * 4,
        scratch_shapes=[dma((4,))],
        compiler_params=pltpu.CompilerParams(vmem_limit_bytes=1 << 20),
        name="deliver",
    )(*results)


def solution(mesh):
    return jax.shard_map(
        local,
        mesh=mesh,
        in_specs=(
            P("dp", "row", "col", None),
            P("dp", "row", "col", None),
            P(("row", "col"), "dp", None),
            P(("row", "col"), "dp", None),
            P(("row", "col"), "dp"),
            P(("row", "col"), "dp"),
        ),
        out_specs=(
            P("dp", "row", "col", None),
            P("dp", "row", "col", None),
            P(("row", "col"), "dp", None),
            P(("row", "col"), "dp", None),
        ),
        check_vma=False,
    )
```

```python
import functools
import math

import jax
import jax.numpy as jnp
from jax import lax
from jax.experimental import pallas as pl
from jax.experimental.pallas import tpu as pltpu
from jax.sharding import PartitionSpec as P

MESH = pl.DeviceIdType.MESH
GAMMA = 1.7015043497085571
ALPHA = 0.2
EPS = 1e-06
G = 128
FAN = 9 * G
ROOT = math.sqrt(FAN)
NY, NZ, NX = 4, 2, 4
MEMBERS = NZ * NX
H, W = 8, 64
PIX = H * W
BF = jnp.bfloat16
F32 = jnp.float32
CUBE = 0.044715
SLOPE = math.sqrt(2 / math.pi)


def gelu_pair(x):
    square = x * x
    t = jnp.tanh(SLOPE * x * (1.0 + CUBE * square))
    half = (0.5 * GAMMA) * (1.0 + t)
    value = half * x
    slope = half + (0.5 * GAMMA * SLOPE) * x * (1.0 - t * t) * (1.0 + (3.0 * CUBE) * square)
    return value, slope


def column(gain):
    n = gain.shape[1]
    eye = lax.broadcasted_iota(jnp.int32, (n, n), 0) == lax.broadcasted_iota(jnp.int32, (n, n), 1)
    return jnp.sum(jnp.where(eye, jnp.broadcast_to(gain, (n, n)), 0.0), axis=1, keepdims=True)


def centre(kernel):
    c = kernel - jnp.mean(kernel, axis=1, keepdims=True)
    r = lax.rsqrt(jnp.mean(c * c, axis=1, keepdims=True) + EPS)
    return c, r


def body(
    feat, cot, k1_hbm, k2_hbm, g1_hbm, g2_hbm,
    out, igrad, kg1, kg2,
    k1, k2, g1, g2, kout1, kout2, cent, p_sem, xin, cin, obuf, ibuf, shard, wall, wf, wa, apad, hpad, gpad, zpad, slope_x, slope_z,
    acc, gsend, grecv, zsend, zrecv,
    in_send, in_recv, w_send, w_recv, o_send, o_recv, g_send, g_recv,
):
    dp, row, col = lax.axis_index("dp"), lax.axis_index("row"), lax.axis_index("col")
    y, m = dp // MEMBERS, dp % MEMBERS
    spot = row * 2 + col
    seat = y * 4 + spot
    group = spot * NY + y

    zh, x = m // NX, m % NX

    def peer(step, p):
        py = lax.rem(y + step, NY)
        return (py * MEMBERS + m, p // 2, p % 2), py

    def along(j):
        return (y * MEMBERS + zh * NX + lax.rem(x + j, NX), row, col)

    other = (1 - zh) * NX + x
    partner = (y * MEMBERS + other, row, col)

    params = [
        pltpu.make_async_copy(s, d, p_sem.at[i])
        for i, (s, d) in enumerate(((k1_hbm, k1), (k2_hbm, k2), (g1_hbm, g1), (g2_hbm, g2)))
    ]
    for copy in params:
        copy.start()
    barrier = pltpu.get_barrier_semaphore()

    @pl.loop(1, 16)
    def _(k):
        step, p = k // 4, lax.rem(spot + k % 4, 4)
        pl.semaphore_signal(barrier, inc=1, device_id=peer(step, p)[0], device_id_type=MESH)

    for j in range(1, NX):
        pl.semaphore_signal(barrier, inc=1, device_id=along(j), device_id_type=MESH)
    pl.semaphore_signal(barrier, inc=1, device_id=partner, device_id_type=MESH)

    for copy in params:
        copy.wait()
    gains = (column(g1[...]), column(g2[...]))
    inverse = []
    for idx, k in enumerate((k1, k2)):
        c, r = centre(k[0])
        inverse.append(r)
        cent[idx] = c
        shard[idx] = (gains[idx] * c * r / ROOT).astype(BF)
    zero = jnp.zeros((W, G), BF)
    for pad in [p.at[n] for p in (apad, hpad, gpad, zpad) for n in range(NY)]:
        pad[0:W] = zero
        pad[W + PIX : 2 * W + PIX] = zero
    acc[...] = jnp.zeros_like(acc)
    empty = jnp.zeros((G, G), BF)
    for idx in range(2):
        for dx in range(3):
            for s in range(2):
                at, gap = (2 * dx + s) * G, (3 - 3 * s) * G
                wf[idx, at : at + G, gap : gap + G] = empty
                wa[idx, gap : gap + G, at : at + G] = empty

    pl.semaphore_wait(barrier, 15 + NX)

    def in_copy(which, step, p):
        src, dst = ((feat, xin), (cot, cin))[which]
        dev, py = peer(step, p)
        lane = pl.multiple_of((p * NY + py) * G, G)
        s = src.at[0, :, :, pl.ds(lane, G)]
        d = dst.at[y, pl.ds(row * 4, 4), pl.ds(pl.multiple_of(col * 32, 32), 32), :]
        return s, d, dev

    def in_remote(which, step, p):
        s, d, dev = in_copy(which, step, p)
        return pltpu.make_async_remote_copy(
            src_ref=s, dst_ref=d, send_sem=in_send.at[which, step, p],
            recv_sem=in_recv.at[which, y], device_id=dev, device_id_type=MESH,
        )

    def own_copy(which):
        s, d, _ = in_copy(which, 0, spot)
        return pltpu.make_async_copy(s, d, in_recv.at[which, y])

    def rows(member):
        return wall.at[:, pl.ds(pl.multiple_of(member * 16, 16), 16), :]

    def w_send_to(idx, src, member, dev, slot, recv):
        return pltpu.make_async_remote_copy(
            src_ref=src.at[idx], dst_ref=rows(member).at[idx], send_sem=w_send.at[idx, slot],
            recv_sem=w_recv.at[idx, recv], device_id=dev, device_id_type=MESH,
        )

    w_across = [w_send_to(idx, shard, m, partner, 0, 0) for idx in range(2)]
    w_first = [[w_send_to(idx, shard, m, along(j), j, 1) for j in range(1, NX)] for idx in range(2)]
    w_second = [
        [w_send_to(idx, rows(other), other, along(j), NX - 1 + j, 1) for j in range(1, NX)]
        for idx in range(2)
    ]
    w_own = pltpu.make_async_copy(shard, rows(m), w_recv.at[0, 2])
    for copy in w_across + w_first[0] + w_first[1] + [w_own]:
        copy.start()
    own_copy(0).start()
    own_copy(1).start()

    def in_start(step, prow):
        for pcol in range(2):
            for which in range(2):
                in_remote(which, step, prow * 2 + pcol).start()

    def in_wait(which, n):
        src = (xin, cin)[which]
        pltpu.make_async_copy(src.at[n], src.at[n], in_recv.at[which, n]).wait()

    for which in range(2):
        in_remote(which, 0, row * 2 + 1 - col).start()
    in_start(0, 1 - row)
    in_start(3, row)
    in_start(1, row)
    in_start(2, row)
    w_across[0].wait_recv()
    for copy in w_second[0]:
        copy.start()
    in_start(3, 1 - row)
    in_start(1, 1 - row)
    in_start(2, 1 - row)
    w_across[1].wait_recv()
    for copy in w_second[1]:
        copy.start()
    w_own.wait()

    def w_ready(idx):
        gathered = wall.at[idx, 0 : 2 * (NX - 1) * 16, :]
        pltpu.make_async_copy(gathered, gathered, w_recv.at[idx, 1]).wait()
        for dx in range(3):
            for s in range(2):
                at = (2 * dx + s) * G
                for dy in range(3):
                    block = wall[idx, :, (3 * dy + dx) * G : (3 * dy + dx + 1) * G]
                    wf[idx, at : at + G, (dy + s) * G : (dy + s + 1) * G] = block
                    wa[idx, (s + 2 - dy) * G : (s + 3 - dy) * G, at : at + G] = block

    where = lax.broadcasted_iota(jnp.int32, (PIX, G), 0) % W
    left, right = where == 0, where == W - 1

    def later(v):
        return jnp.where(left[: v.shape[0]], 0.0, pltpu.roll(v, 1, 0))

    def sooner(v):
        return jnp.where(right[: v.shape[0]], 0.0, pltpu.roll(v, v.shape[0] - 1, 0))

    def stack(pad, order):
        return jnp.concatenate([pad[d * W : d * W + PIX] for d in order], axis=1)

    def pairs(pad):
        return jnp.concatenate(
            [
                jnp.concatenate([pad[(2 * t + r) * W : (2 * t + r + 1) * W] for t in range(H // 2)], axis=0)
                for r in range(4)
            ],
            axis=1,
        )

    def weave(p, before, after):
        rows = []
        for s in range(2):
            part = [p[:, (2 * dx + s) * G : (2 * dx + s + 1) * G] for dx in range(3)]
            rows.append(before(part[0]) + part[1] + after(part[2]))
        return jnp.concatenate(
            [rows[s][t * W : (t + 1) * W] for t in range(H // 2) for s in range(2)], axis=0
        )

    def forward(pad, idx):
        p = lax.dot_general(
            pairs(pad), wf[idx], (((1,), (1,)), ((), ())), preferred_element_type=F32
        )
        return weave(p, later, sooner)

    def adjoint(pad, idx):
        p = jnp.dot(pairs(pad), wa[idx], preferred_element_type=F32)
        return weave(p, sooner, later)

    def terms(v, pad, idx):
        g = jnp.concatenate([sooner(v).astype(BF), v.astype(BF), later(v).astype(BF)], axis=1)
        acc[idx] += lax.dot_general(
            g, stack(pad, (0, 1, 2)), (((0,), (0,)), ((), ())), preferred_element_type=F32
        )

    def out_copy(which, n, p):
        src, dst = ((obuf, out), (ibuf, igrad))[which]
        s = src.at[n, pl.ds(p // 2 * 4, 4), pl.ds(pl.multiple_of(p % 2 * 32, 32), 32), :]
        d = dst.at[0, :, :, pl.ds(pl.multiple_of(group * G, G), G)]
        return s, d

    def out_remote(which, n, p):
        s, d = out_copy(which, n, p)
        return pltpu.make_async_remote_copy(
            src_ref=s, dst_ref=d, send_sem=o_send.at[which, n, p], recv_sem=o_recv.at[which],
            device_id=(n * MEMBERS + m, p // 2, p % 2), device_id_type=MESH,
        )

    def out_list(which, n, own):
        return [out_remote(which, n, lax.rem(spot + k, 4)) for k in range(1 if own else 0, 4)]

    def out_start(which, n, own):
        for copy in out_list(which, n, own):
            copy.start()
        if own:
            s, d = out_copy(which, n, spot)
            pltpu.make_async_copy(s, d, o_recv.at[which]).start()

    def g_along(idx, step):
        return pltpu.make_async_remote_copy(
            src_ref=gsend.at[idx, lax.rem(x + step, NX)], dst_ref=grecv.at[idx, x],
            send_sem=g_send.at[idx, step], recv_sem=g_recv.at[idx, 0],
            device_id=along(step), device_id_type=MESH,
        )

    g_across = [
        pltpu.make_async_remote_copy(
            src_ref=zsend.at[idx], dst_ref=zrecv.at[idx], send_sem=g_send.at[idx, 0],
            recv_sem=g_recv.at[idx, 1], device_id=partner, device_id_type=MESH,
        )
        for idx in range(2)
    ]

    def pack(idx):
        for member in range(MEMBERS):
            for tap in range(9):
                dy, dx = tap // 3, tap % 3
                gsend[idx, member % NX, member // NX, :, tap * G : (tap + 1) * G] = acc[
                    idx, dx * G + member * 16 : dx * G + member * 16 + 16, dy * G : (dy + 1) * G
                ].astype(BF)

    def order(j):
        return lax.rem(y + (0, 1, 3, 2)[j], NY)

    def results(n, own=False):
        res = xin[n].reshape(PIX, G).astype(F32) + ALPHA * forward(hpad.at[n], 1)
        obuf[n] = res.astype(BF).reshape(H, W, G)
        back = adjoint(zpad.at[n], 0)
        out_start(0, n, own)
        ig = cin[n].reshape(PIX, G).astype(F32) + slope_x[n] * back
        ibuf[n] = ig.astype(BF).reshape(H, W, G)
        out_start(1, n, own)

    def arrive(n):
        in_wait(0, n)
        in_wait(1, n)

    def first(n):
        value, slope = gelu_pair(xin[n].reshape(PIX, G).astype(F32))
        slope_x[n] = slope
        apad[n, W : W + PIX] = value.astype(BF)
        gpad[n, W : W + PIX] = (ALPHA * cin[n].reshape(PIX, G).astype(F32)).astype(BF)

    def bend(n):
        z = forward(apad.at[n], 0).astype(BF).astype(F32)
        value, slope = gelu_pair(z)
        hpad[n, W : W + PIX] = value.astype(BF)
        return slope

    def lower(n, slope):
        zpad[n, W : W + PIX] = (adjoint(gpad.at[n], 1) * slope).astype(BF)

    def middle(n):
        dh = adjoint(gpad.at[n], 1)
        slope = bend(n)
        zpad[n, W : W + PIX] = (dh * slope).astype(BF)

    def terms_two(n):
        terms(gpad[n, W : W + PIX].astype(F32), hpad.at[n], 1)

    def terms_one(n):
        terms(zpad[n, W : W + PIX].astype(F32), apad.at[n], 0)

    def along_start(idx):
        for step in range(1, NX):
            g_along(idx, step).start()

    images = [order(j) for j in range(NY)]
    n0, n1, n2, n3 = images
    arrive(n0)
    first(n0)
    w_ready(0)
    slope_z[0] = bend(n0)
    terms_two(n0)
    w_ready(1)
    lower(n0, slope_z[0])
    terms_one(n0)
    results(n0, True)
    arrive(n1)
    first(n1)
    middle(n1)
    terms_two(n1)
    terms_one(n1)
    arrive(n2)
    first(n2)
    results(n1)
    middle(n2)
    terms_two(n2)
    terms_one(n2)
    arrive(n3)
    first(n3)
    slope_z[0] = bend(n3)
    terms_two(n3)
    pack(1)
    along_start(1)
    lower(n3, slope_z[0])
    terms_one(n3)
    pack(0)
    along_start(0)
    results(n2)
    results(n3)

    for step in range(4):
        @pl.loop(0 if step else 1, 4)
        def _(k):
            p = lax.rem(spot + k, 4)
            in_remote(0, step, p).wait_send()
            in_remote(1, step, p).wait_send()

    for copy in w_across + w_first[0] + w_first[1] + w_second[0] + w_second[1]:
        copy.wait_send()
    def summed(half, idx):
        total = gsend[idx, x, half].astype(F32)
        for step in range(1, NX):
            total = total + grecv[idx, lax.rem(x + step, NX), half].astype(F32)
        return total

    mine = {}
    for idx in (1, 0):
        arrived = grecv.at[idx, 0 : NX - 1]
        pltpu.make_async_copy(arrived, arrived, g_recv.at[idx, 0]).wait()
        zsend[idx] = summed(1 - zh, idx).astype(BF)
        mine[idx] = summed(zh, idx)
        g_across[idx].start()
    for n in images:
        for which in range(2):
            for copy in out_list(which, n, n is n0):
                copy.wait_send()
    for idx, kg in ((1, kout2), (0, kout1)):
        g_across[idx].wait_recv()
        total = mine[idx] + zrecv[idx].astype(F32)
        c = cent[idx]
        r = inverse[idx]
        mean_c = jnp.mean(c, axis=1, keepdims=True)
        mean_t = jnp.mean(total, axis=1, keepdims=True)
        pull = r * r * jnp.mean(total * c, axis=1, keepdims=True)
        kg[0] = (gains[idx] * r / ROOT) * ((total - mean_t) - pull * (c - mean_c))
    finals = [
        pltpu.make_async_copy(s, d, p_sem.at[i]) for i, (s, d) in enumerate(((kout1, kg1), (kout2, kg2)))
    ]
    for copy in finals:
        copy.start()

    for idx in range(2):
        g_across[idx].wait_send()
        for step in range(1, NX):
            g_along(idx, step).wait_send()

    for which in range(2):
        dst = (out, igrad)[which]
        pltpu.make_async_copy(dst, dst, o_recv.at[which]).wait()
    for copy in finals:
        copy.wait()


def deliver(a, b, c, d, ao, bo, co, do, sem):
    copies = [
        pltpu.make_async_copy(s, t, sem.at[i])
        for i, (s, t) in enumerate(((a, ao), (b, bo), (c, co), (d, do)))
    ]
    for copy in copies:
        copy.start()
    for copy in copies:
        copy.wait()


def local(features, cotangent, kernel_one, kernel_two, gain_one, gain_two):
    hbm = pl.BlockSpec(memory_space=pltpu.HBM)
    raw = pl.BlockSpec(memory_space=pl.ANY)
    vm = pltpu.VMEM
    dma = pltpu.SemaphoreType.DMA
    shapes = (
        jax.ShapeDtypeStruct(features.shape, BF),
        jax.ShapeDtypeStruct(features.shape, BF),
        jax.ShapeDtypeStruct(kernel_one.shape, F32),
        jax.ShapeDtypeStruct(kernel_two.shape, F32),
    )
    results = pl.pallas_call(
        body,
        out_shape=shapes,
        in_specs=[hbm] * 6,
        out_specs=(raw,) * 4,
        scratch_shapes=[
            vm((1, 16, FAN), F32), vm((1, 16, FAN), F32), vm((1, 16), F32), vm((1, 16), F32),
            vm((1, 16, FAN), F32), vm((1, 16, FAN), F32), vm((2, 16, FAN), F32), dma((4,)),
            vm((NY, H, W, G), BF), vm((NY, H, W, G), BF),
            vm((NY, H, W, G), BF), vm((NY, H, W, G), BF),
            vm((2, 16, FAN), BF), vm((2, G, FAN), BF),
            vm((2, 6 * G, 4 * G), BF), vm((2, 4 * G, 6 * G), BF),
            vm((NY, PIX + 2 * W, G), BF), vm((NY, PIX + 2 * W, G), BF),
            vm((NY, PIX + 2 * W, G), BF), vm((NY, PIX + 2 * W, G), BF),
            vm((NY, PIX, G), F32), vm((1, PIX, G), F32),
            vm((2, 3 * G, 3 * G), F32),
            vm((2, NX, NZ, 16, FAN), BF), vm((2, NX, NZ, 16, FAN), BF),
            vm((2, 16, FAN), BF), vm((2, 16, FAN), BF),
            dma((2, NY, 4)), dma((2, NY)), dma((2, 2 * NX - 1)), dma((2, 3)),
            dma((2, NY, 4)), dma((2,)), dma((2, NX)), dma((2, 2)),
        ],
        compiler_params=pltpu.CompilerParams(
            collective_id=0, has_side_effects=True, vmem_limit_bytes=48 << 20
        ),
        name="block",
    )(*[pltpu.with_memory_space_constraint(v, pltpu.HBM) for v in (features, cotangent, kernel_one, kernel_two, gain_one, gain_two)])
    return pl.pallas_call(
        deliver,
        out_shape=shapes,
        in_specs=[raw] * 4,
        out_specs=(raw,) * 4,
        scratch_shapes=[dma((4,))],
        compiler_params=pltpu.CompilerParams(vmem_limit_bytes=1 << 20),
        name="deliver",
    )(*results)


def solution(mesh):
    return jax.shard_map(
        local,
        mesh=mesh,
        in_specs=(
            P("dp", "row", "col", None),
            P("dp", "row", "col", None),
            P(("row", "col"), "dp", None),
            P(("row", "col"), "dp", None),
            P(("row", "col"), "dp"),
            P(("row", "col"), "dp"),
        ),
        out_specs=(
            P("dp", "row", "col", None),
            P("dp", "row", "col", None),
            P(("row", "col"), "dp", None),
            P(("row", "col"), "dp", None),
        ),
        check_vma=False,
    )
```

```python
import functools
import math

import jax
import jax.numpy as jnp
from jax import lax
from jax.experimental import pallas as pl
from jax.experimental.pallas import tpu as pltpu
from jax.sharding import PartitionSpec as P

MESH = pl.DeviceIdType.MESH
GAMMA = 1.7015043497085571
ALPHA = 0.2
EPS = 1e-06
G = 128
FAN = 9 * G
ROOT = math.sqrt(FAN)
NY, NZ, NX = 4, 2, 4
MEMBERS = NZ * NX
H, W = 8, 64
PIX = H * W
BF = jnp.bfloat16
F32 = jnp.float32
CUBE = 0.044715
SLOPE = math.sqrt(2 / math.pi)


def gelu_pair(x):
    square = x * x
    t = jnp.tanh(SLOPE * x * (1.0 + CUBE * square))
    half = (0.5 * GAMMA) * (1.0 + t)
    value = half * x
    slope = half + (0.5 * GAMMA * SLOPE) * x * (1.0 - t * t) * (1.0 + (3.0 * CUBE) * square)
    return value, slope


def column(gain):
    n = gain.shape[1]
    eye = lax.broadcasted_iota(jnp.int32, (n, n), 0) == lax.broadcasted_iota(jnp.int32, (n, n), 1)
    return jnp.sum(jnp.where(eye, jnp.broadcast_to(gain, (n, n)), 0.0), axis=1, keepdims=True)


def centre(kernel):
    c = kernel - jnp.mean(kernel, axis=1, keepdims=True)
    r = lax.rsqrt(jnp.mean(c * c, axis=1, keepdims=True) + EPS)
    return c, r


def body(
    feat, cot, k1_hbm, k2_hbm, g1_hbm, g2_hbm,
    out, igrad, kg1, kg2,
    k1, k2, g1, g2, kout1, kout2, cent, p_sem, xin, cin, obuf, ibuf, shard, wall, wf, wa, apad, hpad, gpad, zpad, slope_x, slope_z,
    acc, gsend, grecv, zsend, zrecv,
    in_send, in_recv, w_send, w_recv, o_send, o_recv, g_send, g_recv,
):
    dp, row, col = lax.axis_index("dp"), lax.axis_index("row"), lax.axis_index("col")
    y, m = dp // MEMBERS, dp % MEMBERS
    spot = row * 2 + col
    seat = y * 4 + spot
    group = spot * NY + y

    zh, x = m // NX, m % NX

    def peer(step, p):
        py = lax.rem(y + step, NY)
        return (py * MEMBERS + m, p // 2, p % 2), py

    def along(j):
        return (y * MEMBERS + zh * NX + lax.rem(x + j, NX), row, col)

    other = (1 - zh) * NX + x
    partner = (y * MEMBERS + other, row, col)

    params = [
        pltpu.make_async_copy(s, d, p_sem.at[i])
        for i, (s, d) in enumerate(((k1_hbm, k1), (k2_hbm, k2), (g1_hbm, g1), (g2_hbm, g2)))
    ]
    for copy in params:
        copy.start()
    barrier = pltpu.get_barrier_semaphore()

    for device in [partner] + [along(j) for j in (2, 1, 3)]:
        pl.semaphore_signal(barrier, inc=1, device_id=device, device_id_type=MESH)
    for step in (2, 1, 3, 0):
        for k in (2, 3, 1, 0) if step else (2, 3, 1):
            device = peer(step, lax.rem(spot + k, 4))[0]
            pl.semaphore_signal(barrier, inc=1, device_id=device, device_id_type=MESH)

    for copy in params:
        copy.wait()
    gains = (column(g1[...]), column(g2[...]))
    inverse = []
    for idx, k in enumerate((k1, k2)):
        c, r = centre(k[0])
        inverse.append(r)
        cent[idx] = c
        shard[idx] = (gains[idx] * c * r / ROOT).astype(BF)
    zero = jnp.zeros((W, G), BF)
    for pad in [p.at[n] for p in (apad, hpad, gpad, zpad) for n in range(NY)]:
        pad[0:W] = zero
        pad[W + PIX : 2 * W + PIX] = zero
    acc[...] = jnp.zeros_like(acc)
    empty = jnp.zeros((G, G), BF)
    for idx in range(2):
        for dx in range(3):
            for s in range(2):
                at, gap = (2 * dx + s) * G, (3 - 3 * s) * G
                wf[idx, at : at + G, gap : gap + G] = empty
                wa[idx, gap : gap + G, at : at + G] = empty

    pl.semaphore_wait(barrier, 15 + NX)

    def in_copy(which, step, p):
        src, dst = ((feat, xin), (cot, cin))[which]
        dev, py = peer(step, p)
        lane = pl.multiple_of((p * NY + py) * G, G)
        s = src.at[0, :, :, pl.ds(lane, G)]
        d = dst.at[y, pl.ds(row * 4, 4), pl.ds(pl.multiple_of(col * 32, 32), 32), :]
        return s, d, dev

    def in_remote(which, step, p):
        s, d, dev = in_copy(which, step, p)
        return pltpu.make_async_remote_copy(
            src_ref=s, dst_ref=d, send_sem=in_send.at[which, step, p],
            recv_sem=in_recv.at[which, y], device_id=dev, device_id_type=MESH,
        )

    def own_copy(which):
        s, d, _ = in_copy(which, 0, spot)
        return pltpu.make_async_copy(s, d, in_recv.at[which, y])

    def rows(member):
        return wall.at[:, pl.ds(pl.multiple_of(member * 16, 16), 16), :]

    def w_send_to(idx, src, member, dev, slot, recv):
        return pltpu.make_async_remote_copy(
            src_ref=src.at[idx], dst_ref=rows(member).at[idx], send_sem=w_send.at[idx, slot],
            recv_sem=w_recv.at[idx, recv], device_id=dev, device_id_type=MESH,
        )

    w_across = [w_send_to(idx, shard, m, partner, 0, 0) for idx in range(2)]
    w_first = [[w_send_to(idx, shard, m, along(j), j, 1) for j in range(1, NX)] for idx in range(2)]
    w_second = [
        [w_send_to(idx, rows(other), other, along(j), NX - 1 + j, 1) for j in range(1, NX)]
        for idx in range(2)
    ]
    w_own = pltpu.make_async_copy(shard, rows(m), w_recv.at[0, 2])
    for copy in w_across + w_first[0] + w_first[1] + [w_own]:
        copy.start()
    own_copy(0).start()
    own_copy(1).start()

    def in_start(step, prow):
        for pcol in range(2):
            for which in range(2):
                in_remote(which, step, prow * 2 + pcol).start()

    def in_wait(which, n):
        src = (xin, cin)[which]
        pltpu.make_async_copy(src.at[n], src.at[n], in_recv.at[which, n]).wait()

    for which in range(2):
        in_remote(which, 0, row * 2 + 1 - col).start()
    in_start(0, 1 - row)
    in_start(3, row)
    in_start(1, row)
    in_start(2, row)
    w_across[0].wait_recv()
    for copy in w_second[0]:
        copy.start()
    in_start(3, 1 - row)
    in_start(1, 1 - row)
    in_start(2, 1 - row)
    w_across[1].wait_recv()
    for copy in w_second[1]:
        copy.start()
    w_own.wait()

    def w_ready(idx):
        gathered = wall.at[idx, 0 : 2 * (NX - 1) * 16, :]
        pltpu.make_async_copy(gathered, gathered, w_recv.at[idx, 1]).wait()
        for dx in range(3):
            for s in range(2):
                at = (2 * dx + s) * G
                for dy in range(3):
                    block = wall[idx, :, (3 * dy + dx) * G : (3 * dy + dx + 1) * G]
                    wf[idx, at : at + G, (dy + s) * G : (dy + s + 1) * G] = block
                    wa[idx, (s + 2 - dy) * G : (s + 3 - dy) * G, at : at + G] = block

    where = lax.broadcasted_iota(jnp.int32, (PIX, G), 0) % W
    left, right = where == 0, where == W - 1

    def later(v):
        return jnp.where(left[: v.shape[0]], 0.0, pltpu.roll(v, 1, 0))

    def sooner(v):
        return jnp.where(right[: v.shape[0]], 0.0, pltpu.roll(v, v.shape[0] - 1, 0))

    def stack(pad, order):
        return jnp.concatenate([pad[d * W : d * W + PIX] for d in order], axis=1)

    def pairs(pad):
        return jnp.concatenate(
            [
                jnp.concatenate([pad[(2 * t + r) * W : (2 * t + r + 1) * W] for t in range(H // 2)], axis=0)
                for r in range(4)
            ],
            axis=1,
        )

    def weave(p, before, after):
        rows = []
        for s in range(2):
            part = [p[:, (2 * dx + s) * G : (2 * dx + s + 1) * G] for dx in range(3)]
            rows.append(before(part[0]) + part[1] + after(part[2]))
        return jnp.concatenate(
            [rows[s][t * W : (t + 1) * W] for t in range(H // 2) for s in range(2)], axis=0
        )

    def forward(pad, idx):
        p = lax.dot_general(
            pairs(pad), wf[idx], (((1,), (1,)), ((), ())), preferred_element_type=F32
        )
        return weave(p, later, sooner)

    def adjoint(pad, idx):
        p = jnp.dot(pairs(pad), wa[idx], preferred_element_type=F32)
        return weave(p, sooner, later)

    def terms(v, pad, idx):
        g = jnp.concatenate([sooner(v).astype(BF), v.astype(BF), later(v).astype(BF)], axis=1)
        acc[idx] += lax.dot_general(
            g, stack(pad, (0, 1, 2)), (((0,), (0,)), ((), ())), preferred_element_type=F32
        )

    def out_copy(which, n, p):
        src, dst = ((obuf, out), (ibuf, igrad))[which]
        s = src.at[n, pl.ds(p // 2 * 4, 4), pl.ds(pl.multiple_of(p % 2 * 32, 32), 32), :]
        d = dst.at[0, :, :, pl.ds(pl.multiple_of(group * G, G), G)]
        return s, d

    def out_remote(which, n, p):
        s, d = out_copy(which, n, p)
        return pltpu.make_async_remote_copy(
            src_ref=s, dst_ref=d, send_sem=o_send.at[which, n, p], recv_sem=o_recv.at[which],
            device_id=(n * MEMBERS + m, p // 2, p % 2), device_id_type=MESH,
        )

    def out_list(which, n, own):
        return [out_remote(which, n, lax.rem(spot + k, 4)) for k in range(1 if own else 0, 4)]

    def out_start(which, n, own):
        for copy in out_list(which, n, own):
            copy.start()
        if own:
            s, d = out_copy(which, n, spot)
            pltpu.make_async_copy(s, d, o_recv.at[which]).start()

    def g_along(idx, step):
        return pltpu.make_async_remote_copy(
            src_ref=gsend.at[idx, lax.rem(x + step, NX)], dst_ref=grecv.at[idx, x],
            send_sem=g_send.at[idx, step], recv_sem=g_recv.at[idx, 0],
            device_id=along(step), device_id_type=MESH,
        )

    g_across = [
        pltpu.make_async_remote_copy(
            src_ref=zsend.at[idx], dst_ref=zrecv.at[idx], send_sem=g_send.at[idx, 0],
            recv_sem=g_recv.at[idx, 1], device_id=partner, device_id_type=MESH,
        )
        for idx in range(2)
    ]

    def pack(idx):
        for member in range(MEMBERS):
            for tap in range(9):
                dy, dx = tap // 3, tap % 3
                gsend[idx, member % NX, member // NX, :, tap * G : (tap + 1) * G] = acc[
                    idx, dx * G + member * 16 : dx * G + member * 16 + 16, dy * G : (dy + 1) * G
                ].astype(BF)

    def order(j):
        return lax.rem(y + (0, 1, 3, 2)[j], NY)

    def results(n, own=False):
        res = xin[n].reshape(PIX, G).astype(F32) + ALPHA * forward(hpad.at[n], 1)
        obuf[n] = res.astype(BF).reshape(H, W, G)
        back = adjoint(zpad.at[n], 0)
        out_start(0, n, own)
        ig = cin[n].reshape(PIX, G).astype(F32) + slope_x[n] * back
        ibuf[n] = ig.astype(BF).reshape(H, W, G)
        out_start(1, n, own)

    def arrive(n):
        in_wait(0, n)
        in_wait(1, n)

    def first(n):
        value, slope = gelu_pair(xin[n].reshape(PIX, G).astype(F32))
        slope_x[n] = slope
        apad[n, W : W + PIX] = value.astype(BF)
        gpad[n, W : W + PIX] = (ALPHA * cin[n].reshape(PIX, G).astype(F32)).astype(BF)

    def bend(n):
        z = forward(apad.at[n], 0).astype(BF).astype(F32)
        value, slope = gelu_pair(z)
        hpad[n, W : W + PIX] = value.astype(BF)
        return slope

    def lower(n, slope):
        zpad[n, W : W + PIX] = (adjoint(gpad.at[n], 1) * slope).astype(BF)

    def middle(n):
        dh = adjoint(gpad.at[n], 1)
        slope = bend(n)
        zpad[n, W : W + PIX] = (dh * slope).astype(BF)

    def terms_two(n):
        terms(gpad[n, W : W + PIX].astype(F32), hpad.at[n], 1)

    def terms_one(n):
        terms(zpad[n, W : W + PIX].astype(F32), apad.at[n], 0)

    def along_start(idx):
        for step in range(1, NX):
            g_along(idx, step).start()

    images = [order(j) for j in range(NY)]
    n0, n1, n2, n3 = images
    arrive(n0)
    first(n0)
    w_ready(0)
    slope_z[0] = bend(n0)
    terms_two(n0)
    w_ready(1)
    lower(n0, slope_z[0])
    terms_one(n0)
    results(n0, True)
    arrive(n1)
    first(n1)
    middle(n1)
    terms_two(n1)
    terms_one(n1)
    arrive(n2)
    first(n2)
    results(n1)
    middle(n2)
    terms_two(n2)
    terms_one(n2)
    arrive(n3)
    first(n3)
    slope_z[0] = bend(n3)
    terms_two(n3)
    pack(1)
    along_start(1)
    lower(n3, slope_z[0])
    terms_one(n3)
    pack(0)
    along_start(0)
    results(n2)
    results(n3)

    for step in range(4):
        @pl.loop(0 if step else 1, 4)
        def _(k):
            p = lax.rem(spot + k, 4)
            in_remote(0, step, p).wait_send()
            in_remote(1, step, p).wait_send()

    for copy in w_across + w_first[0] + w_first[1] + w_second[0] + w_second[1]:
        copy.wait_send()
    def summed(half, idx):
        total = gsend[idx, x, half].astype(F32)
        for step in range(1, NX):
            total = total + grecv[idx, lax.rem(x + step, NX), half].astype(F32)
        return total

    mine = {}
    for idx in (1, 0):
        arrived = grecv.at[idx, 0 : NX - 1]
        pltpu.make_async_copy(arrived, arrived, g_recv.at[idx, 0]).wait()
        zsend[idx] = summed(1 - zh, idx).astype(BF)
        mine[idx] = summed(zh, idx)
        g_across[idx].start()
    for n in images:
        for which in range(2):
            for copy in out_list(which, n, n is n0):
                copy.wait_send()
    finals = []
    for idx, kg, target in ((1, kout2, kg2), (0, kout1, kg1)):
        g_across[idx].wait_recv()
        total = mine[idx] + zrecv[idx].astype(F32)
        c = cent[idx]
        r = inverse[idx]
        mean_c = jnp.mean(c, axis=1, keepdims=True)
        mean_t = jnp.mean(total, axis=1, keepdims=True)
        pull = r * r * jnp.mean(total * c, axis=1, keepdims=True)
        kg[0] = (gains[idx] * r / ROOT) * ((total - mean_t) - pull * (c - mean_c))
        finals.append(pltpu.make_async_copy(kg, target, p_sem.at[idx]))
        finals[-1].start()
    for idx in range(2):
        g_across[idx].wait_send()
        for step in range(1, NX):
            g_along(idx, step).wait_send()

    for which in range(2):
        dst = (out, igrad)[which]
        pltpu.make_async_copy(dst, dst, o_recv.at[which]).wait()
    for copy in finals:
        copy.wait()


def deliver(a, b, c, d, ao, bo, co, do, sem):
    copies = [
        pltpu.make_async_copy(s, t, sem.at[i])
        for i, (s, t) in enumerate(((a, ao), (b, bo), (c, co), (d, do)))
    ]
    for copy in copies:
        copy.start()
    for copy in copies:
        copy.wait()


def local(features, cotangent, kernel_one, kernel_two, gain_one, gain_two):
    hbm = pl.BlockSpec(memory_space=pltpu.HBM)
    raw = pl.BlockSpec(memory_space=pl.ANY)
    vm = pltpu.VMEM
    dma = pltpu.SemaphoreType.DMA
    shapes = (
        jax.ShapeDtypeStruct(features.shape, BF),
        jax.ShapeDtypeStruct(features.shape, BF),
        jax.ShapeDtypeStruct(kernel_one.shape, F32),
        jax.ShapeDtypeStruct(kernel_two.shape, F32),
    )
    results = pl.pallas_call(
        body,
        out_shape=shapes,
        in_specs=[hbm] * 6,
        out_specs=(raw,) * 4,
        scratch_shapes=[
            vm((1, 16, FAN), F32), vm((1, 16, FAN), F32), vm((1, 16), F32), vm((1, 16), F32),
            vm((1, 16, FAN), F32), vm((1, 16, FAN), F32), vm((2, 16, FAN), F32), dma((4,)),
            vm((NY, H, W, G), BF), vm((NY, H, W, G), BF),
            vm((NY, H, W, G), BF), vm((NY, H, W, G), BF),
            vm((2, 16, FAN), BF), vm((2, G, FAN), BF),
            vm((2, 6 * G, 4 * G), BF), vm((2, 4 * G, 6 * G), BF),
            vm((NY, PIX + 2 * W, G), BF), vm((NY, PIX + 2 * W, G), BF),
            vm((NY, PIX + 2 * W, G), BF), vm((NY, PIX + 2 * W, G), BF),
            vm((NY, PIX, G), F32), vm((1, PIX, G), F32),
            vm((2, 3 * G, 3 * G), F32),
            vm((2, NX, NZ, 16, FAN), BF), vm((2, NX, NZ, 16, FAN), BF),
            vm((2, 16, FAN), BF), vm((2, 16, FAN), BF),
            dma((2, NY, 4)), dma((2, NY)), dma((2, 2 * NX - 1)), dma((2, 3)),
            dma((2, NY, 4)), dma((2,)), dma((2, NX)), dma((2, 2)),
        ],
        compiler_params=pltpu.CompilerParams(
            collective_id=0, has_side_effects=True, vmem_limit_bytes=48 << 20
        ),
        name="block",
    )(*[pltpu.with_memory_space_constraint(v, pltpu.HBM) for v in (features, cotangent, kernel_one, kernel_two, gain_one, gain_two)])
    return pl.pallas_call(
        deliver,
        out_shape=shapes,
        in_specs=[raw] * 4,
        out_specs=(raw,) * 4,
        scratch_shapes=[dma((4,))],
        compiler_params=pltpu.CompilerParams(vmem_limit_bytes=1 << 20),
        name="deliver",
    )(*results)


def solution(mesh):
    return jax.shard_map(
        local,
        mesh=mesh,
        in_specs=(
            P("dp", "row", "col", None),
            P("dp", "row", "col", None),
            P(("row", "col"), "dp", None),
            P(("row", "col"), "dp", None),
            P(("row", "col"), "dp"),
            P(("row", "col"), "dp"),
        ),
        out_specs=(
            P("dp", "row", "col", None),
            P("dp", "row", "col", None),
            P(("row", "col"), "dp", None),
            P(("row", "col"), "dp", None),
        ),
        check_vma=False,
    )
```

```python
import functools
import math

import jax
import jax.numpy as jnp
from jax import lax
from jax.experimental import pallas as pl
from jax.experimental.pallas import tpu as pltpu
from jax.sharding import PartitionSpec as P

MESH = pl.DeviceIdType.MESH
GAMMA = 1.7015043497085571
ALPHA = 0.2
EPS = 1e-06
G = 128
FAN = 9 * G
ROOT = math.sqrt(FAN)
NY, NZ, NX = 4, 2, 4
MEMBERS = NZ * NX
H, W = 8, 64
PIX = H * W
BF = jnp.bfloat16
F32 = jnp.float32
CUBE = 0.044715
SLOPE = math.sqrt(2 / math.pi)


def gelu_pair(x):
    square = x * x
    t = jnp.tanh(x * (SLOPE + (SLOPE * CUBE) * square))
    half = 0.5 * GAMMA + (0.5 * GAMMA) * t
    value = half * x
    slope = half + half * ((1.0 - t) * (x * (SLOPE + (3.0 * SLOPE * CUBE) * square)))
    return value, slope


def column(gain):
    n = gain.shape[1]
    eye = lax.broadcasted_iota(jnp.int32, (n, n), 0) == lax.broadcasted_iota(jnp.int32, (n, n), 1)
    return jnp.sum(jnp.where(eye, jnp.broadcast_to(gain, (n, n)), 0.0), axis=1, keepdims=True)


def centre(kernel):
    c = kernel - jnp.mean(kernel, axis=1, keepdims=True)
    r = lax.rsqrt(jnp.mean(c * c, axis=1, keepdims=True) + EPS)
    return c, r


def body(
    feat, cot, k1_hbm, k2_hbm, g1_hbm, g2_hbm,
    out, igrad, kg1, kg2,
    k1, k2, g1, g2, kout1, kout2, cent, p_sem, xin, cin, obuf, ibuf, shard, wall, wf, wa, apad, hpad, gpad, zpad, slope_x, slope_z,
    acc, gsend, grecv, zsend, zrecv,
    in_send, in_recv, w_send, w_recv, o_send, o_recv, g_send, g_recv,
):
    dp, row, col = lax.axis_index("dp"), lax.axis_index("row"), lax.axis_index("col")
    y, m = dp // MEMBERS, dp % MEMBERS
    spot = row * 2 + col
    seat = y * 4 + spot
    group = spot * NY + y

    zh, x = m // NX, m % NX

    def peer(step, p):
        py = lax.rem(y + step, NY)
        return (py * MEMBERS + m, p // 2, p % 2), py

    def along(j):
        return (y * MEMBERS + zh * NX + lax.rem(x + j, NX), row, col)

    other = (1 - zh) * NX + x
    partner = (y * MEMBERS + other, row, col)

    params = [
        pltpu.make_async_copy(s, d, p_sem.at[i])
        for i, (s, d) in enumerate(((k1_hbm, k1), (k2_hbm, k2), (g1_hbm, g1), (g2_hbm, g2)))
    ]
    for copy in params:
        copy.start()
    barrier = pltpu.get_barrier_semaphore()

    for device in [partner] + [along(j) for j in (2, 1, 3)]:
        pl.semaphore_signal(barrier, inc=1, device_id=device, device_id_type=MESH)
    for step in (2, 1, 3, 0):
        for k in (2, 3, 1, 0) if step else (2, 3, 1):
            device = peer(step, lax.rem(spot + k, 4))[0]
            pl.semaphore_signal(barrier, inc=1, device_id=device, device_id_type=MESH)

    for copy in params:
        copy.wait()
    gains = (column(g1[...]), column(g2[...]))
    inverse = []
    for idx, k in enumerate((k1, k2)):
        c, r = centre(k[0])
        inverse.append(r)
        cent[idx] = c
        shard[idx] = (gains[idx] * c * r / ROOT).astype(BF)
    zero = jnp.zeros((W, G), BF)
    for pad in [p.at[n] for p in (apad, hpad, gpad, zpad) for n in range(NY)]:
        pad[0:W] = zero
        pad[W + PIX : 2 * W + PIX] = zero
    acc[...] = jnp.zeros_like(acc)
    empty = jnp.zeros((G, G), BF)
    for idx in range(2):
        for dx in range(3):
            for s in range(2):
                at, gap = (2 * dx + s) * G, (3 - 3 * s) * G
                wf[idx, at : at + G, gap : gap + G] = empty
                wa[idx, gap : gap + G, at : at + G] = empty

    pl.semaphore_wait(barrier, 15 + NX)

    def in_copy(which, step, p):
        src, dst = ((feat, xin), (cot, cin))[which]
        dev, py = peer(step, p)
        lane = pl.multiple_of((p * NY + py) * G, G)
        s = src.at[0, :, :, pl.ds(lane, G)]
        d = dst.at[y, pl.ds(row * 4, 4), pl.ds(pl.multiple_of(col * 32, 32), 32), :]
        return s, d, dev

    def in_remote(which, step, p):
        s, d, dev = in_copy(which, step, p)
        return pltpu.make_async_remote_copy(
            src_ref=s, dst_ref=d, send_sem=in_send.at[which, step, p],
            recv_sem=in_recv.at[which, y], device_id=dev, device_id_type=MESH,
        )

    def own_copy(which):
        s, d, _ = in_copy(which, 0, spot)
        return pltpu.make_async_copy(s, d, in_recv.at[which, y])

    def rows(member):
        return wall.at[:, pl.ds(pl.multiple_of(member * 16, 16), 16), :]

    def w_send_to(idx, src, member, dev, slot, recv):
        return pltpu.make_async_remote_copy(
            src_ref=src.at[idx], dst_ref=rows(member).at[idx], send_sem=w_send.at[idx, slot],
            recv_sem=w_recv.at[idx, recv], device_id=dev, device_id_type=MESH,
        )

    w_across = [w_send_to(idx, shard, m, partner, 0, 0) for idx in range(2)]
    w_first = [[w_send_to(idx, shard, m, along(j), j, 1) for j in range(1, NX)] for idx in range(2)]
    w_second = [
        [w_send_to(idx, rows(other), other, along(j), NX - 1 + j, 1) for j in range(1, NX)]
        for idx in range(2)
    ]
    w_own = pltpu.make_async_copy(shard, rows(m), w_recv.at[0, 2])
    for copy in w_across + w_first[0] + w_first[1]:
        copy.start()

    def in_start(step, prow):
        for pcol in range(2):
            for which in range(2):
                in_remote(which, step, prow * 2 + pcol).start()

    def in_wait(which, n):
        src = (xin, cin)[which]
        pltpu.make_async_copy(src.at[n], src.at[n], in_recv.at[which, n]).wait()

    for which in range(2):
        in_remote(which, 0, row * 2 + 1 - col).start()
    in_start(0, 1 - row)
    in_start(3, row)
    in_start(1, row)
    in_start(2, row)
    w_own.start()
    own_copy(0).start()
    own_copy(1).start()
    w_across[0].wait_recv()
    for copy in w_second[0]:
        copy.start()
    in_start(3, 1 - row)
    in_start(1, 1 - row)
    in_start(2, 1 - row)
    w_across[1].wait_recv()
    for copy in w_second[1]:
        copy.start()
    w_own.wait()

    def w_ready(idx):
        gathered = wall.at[idx, 0 : 2 * (NX - 1) * 16, :]
        pltpu.make_async_copy(gathered, gathered, w_recv.at[idx, 1]).wait()
        for dx in range(3):
            for s in range(2):
                at = (2 * dx + s) * G
                for dy in range(3):
                    block = wall[idx, :, (3 * dy + dx) * G : (3 * dy + dx + 1) * G]
                    wf[idx, at : at + G, (dy + s) * G : (dy + s + 1) * G] = block
                    wa[idx, (s + 2 - dy) * G : (s + 3 - dy) * G, at : at + G] = block

    where = lax.broadcasted_iota(jnp.int32, (PIX, G), 0) % W
    left, right = where == 0, where == W - 1

    def later(v):
        return jnp.where(left[: v.shape[0]], 0.0, pltpu.roll(v, 1, 0))

    def sooner(v):
        return jnp.where(right[: v.shape[0]], 0.0, pltpu.roll(v, v.shape[0] - 1, 0))

    def stack(pad, order):
        return jnp.concatenate([pad[d * W : d * W + PIX] for d in order], axis=1)

    def pairs(pad):
        return jnp.concatenate(
            [
                jnp.concatenate([pad[(2 * t + r) * W : (2 * t + r + 1) * W] for t in range(H // 2)], axis=0)
                for r in range(4)
            ],
            axis=1,
        )

    def weave(p, before, after):
        rows = []
        for s in range(2):
            part = [p[:, (2 * dx + s) * G : (2 * dx + s + 1) * G] for dx in range(3)]
            rows.append(before(part[0]) + part[1] + after(part[2]))
        return jnp.concatenate(
            [rows[s][t * W : (t + 1) * W] for t in range(H // 2) for s in range(2)], axis=0
        )

    def forward(pad, idx):
        p = lax.dot_general(
            pairs(pad), wf[idx], (((1,), (1,)), ((), ())), preferred_element_type=F32
        )
        return weave(p, later, sooner)

    def adjoint(pad, idx):
        p = jnp.dot(pairs(pad), wa[idx], preferred_element_type=F32)
        return weave(p, sooner, later)

    def terms(v, pad, idx):
        g = jnp.concatenate([sooner(v).astype(BF), v.astype(BF), later(v).astype(BF)], axis=1)
        acc[idx] += lax.dot_general(
            g, stack(pad, (0, 1, 2)), (((0,), (0,)), ((), ())), preferred_element_type=F32
        )

    def out_copy(which, n, p):
        src, dst = ((obuf, out), (ibuf, igrad))[which]
        s = src.at[n, pl.ds(p // 2 * 4, 4), pl.ds(pl.multiple_of(p % 2 * 32, 32), 32), :]
        d = dst.at[0, :, :, pl.ds(pl.multiple_of(group * G, G), G)]
        return s, d

    def out_remote(which, n, p):
        s, d = out_copy(which, n, p)
        return pltpu.make_async_remote_copy(
            src_ref=s, dst_ref=d, send_sem=o_send.at[which, n, p], recv_sem=o_recv.at[which],
            device_id=(n * MEMBERS + m, p // 2, p % 2), device_id_type=MESH,
        )

    def out_list(which, n, own):
        return [out_remote(which, n, lax.rem(spot + k, 4)) for k in range(1 if own else 0, 4)]

    def out_start(which, n, own):
        for copy in out_list(which, n, own):
            copy.start()
        if own:
            s, d = out_copy(which, n, spot)
            pltpu.make_async_copy(s, d, o_recv.at[which]).start()

    def g_along(idx, step):
        return pltpu.make_async_remote_copy(
            src_ref=gsend.at[idx, lax.rem(x + step, NX)], dst_ref=grecv.at[idx, x],
            send_sem=g_send.at[idx, step], recv_sem=g_recv.at[idx, 0],
            device_id=along(step), device_id_type=MESH,
        )

    g_across = [
        pltpu.make_async_remote_copy(
            src_ref=zsend.at[idx], dst_ref=zrecv.at[idx], send_sem=g_send.at[idx, 0],
            recv_sem=g_recv.at[idx, 1], device_id=partner, device_id_type=MESH,
        )
        for idx in range(2)
    ]

    def pack(idx):
        for member in range(MEMBERS):
            for tap in range(9):
                dy, dx = tap // 3, tap % 3
                gsend[idx, member % NX, member // NX, :, tap * G : (tap + 1) * G] = acc[
                    idx, dx * G + member * 16 : dx * G + member * 16 + 16, dy * G : (dy + 1) * G
                ].astype(BF)

    def order(j):
        return lax.rem(y + (0, 1, 3, 2)[j], NY)

    def results(n, own=False):
        res = xin[n].reshape(PIX, G).astype(F32) + ALPHA * forward(hpad.at[n], 1)
        obuf[n] = res.astype(BF).reshape(H, W, G)
        back = adjoint(zpad.at[n], 0)
        out_start(0, n, own)
        ig = cin[n].reshape(PIX, G).astype(F32) + slope_x[n] * back
        ibuf[n] = ig.astype(BF).reshape(H, W, G)
        out_start(1, n, own)

    def arrive(n):
        in_wait(0, n)
        in_wait(1, n)

    def first(n):
        value, slope = gelu_pair(xin[n].reshape(PIX, G).astype(F32))
        slope_x[n] = slope
        apad[n, W : W + PIX] = value.astype(BF)
        gpad[n, W : W + PIX] = (ALPHA * cin[n].reshape(PIX, G).astype(F32)).astype(BF)

    def bend(n):
        z = forward(apad.at[n], 0).astype(BF).astype(F32)
        value, slope = gelu_pair(z)
        hpad[n, W : W + PIX] = value.astype(BF)
        return slope

    def lower(n, slope):
        zpad[n, W : W + PIX] = (adjoint(gpad.at[n], 1) * slope).astype(BF)

    def middle(n):
        dh = adjoint(gpad.at[n], 1)
        slope = bend(n)
        zpad[n, W : W + PIX] = (dh * slope).astype(BF)

    def terms_two(n):
        terms(gpad[n, W : W + PIX].astype(F32), hpad.at[n], 1)

    def terms_one(n):
        terms(zpad[n, W : W + PIX].astype(F32), apad.at[n], 0)

    def along_start(idx):
        for step in range(1, NX):
            g_along(idx, step).start()

    images = [order(j) for j in range(NY)]
    n0, n1, n2, n3 = images
    arrive(n0)
    first(n0)
    w_ready(0)
    slope_z[0] = bend(n0)
    terms_two(n0)
    w_ready(1)
    lower(n0, slope_z[0])
    terms_one(n0)
    results(n0, True)
    arrive(n1)
    first(n1)
    middle(n1)
    terms_two(n1)
    terms_one(n1)
    arrive(n2)
    first(n2)
    results(n1)
    middle(n2)
    terms_two(n2)
    terms_one(n2)
    arrive(n3)
    first(n3)
    slope_z[0] = bend(n3)
    terms_two(n3)
    pack(1)
    along_start(1)
    lower(n3, slope_z[0])
    terms_one(n3)
    pack(0)
    along_start(0)
    results(n2)
    results(n3)

    for step in range(4):
        @pl.loop(0 if step else 1, 4)
        def _(k):
            p = lax.rem(spot + k, 4)
            in_remote(0, step, p).wait_send()
            in_remote(1, step, p).wait_send()

    for copy in w_across + w_first[0] + w_first[1] + w_second[0] + w_second[1]:
        copy.wait_send()
    def summed(half, idx):
        total = gsend[idx, x, half].astype(F32)
        for step in range(1, NX):
            total = total + grecv[idx, lax.rem(x + step, NX), half].astype(F32)
        return total

    mine = {}
    for idx in (1, 0):
        arrived = grecv.at[idx, 0 : NX - 1]
        pltpu.make_async_copy(arrived, arrived, g_recv.at[idx, 0]).wait()
        zsend[idx] = summed(1 - zh, idx).astype(BF)
        mine[idx] = summed(zh, idx)
        g_across[idx].start()
    for n in images:
        for which in range(2):
            for copy in out_list(which, n, n is n0):
                copy.wait_send()
    finals = []
    for idx, kg, target in ((1, kout2, kg2), (0, kout1, kg1)):
        g_across[idx].wait_recv()
        total = mine[idx] + zrecv[idx].astype(F32)
        c = cent[idx]
        r = inverse[idx]
        mean_c = jnp.mean(c, axis=1, keepdims=True)
        mean_t = jnp.mean(total, axis=1, keepdims=True)
        pull = r * r * jnp.mean(total * c, axis=1, keepdims=True)
        kg[0] = (gains[idx] * r / ROOT) * ((total - mean_t) - pull * (c - mean_c))
        finals.append(pltpu.make_async_copy(kg, target, p_sem.at[idx]))
        finals[-1].start()
    for idx in range(2):
        g_across[idx].wait_send()
        for step in range(1, NX):
            g_along(idx, step).wait_send()

    for which in range(2):
        dst = (out, igrad)[which]
        pltpu.make_async_copy(dst, dst, o_recv.at[which]).wait()
    for copy in finals:
        copy.wait()


def deliver(a, b, c, d, ao, bo, co, do, sem):
    copies = [
        pltpu.make_async_copy(s, t, sem.at[i])
        for i, (s, t) in enumerate(((a, ao), (b, bo), (c, co), (d, do)))
    ]
    for copy in copies:
        copy.start()
    for copy in copies:
        copy.wait()


def local(features, cotangent, kernel_one, kernel_two, gain_one, gain_two):
    hbm = pl.BlockSpec(memory_space=pltpu.HBM)
    raw = pl.BlockSpec(memory_space=pl.ANY)
    vm = pltpu.VMEM
    dma = pltpu.SemaphoreType.DMA
    shapes = (
        jax.ShapeDtypeStruct(features.shape, BF),
        jax.ShapeDtypeStruct(features.shape, BF),
        jax.ShapeDtypeStruct(kernel_one.shape, F32),
        jax.ShapeDtypeStruct(kernel_two.shape, F32),
    )
    results = pl.pallas_call(
        body,
        out_shape=shapes,
        in_specs=[hbm] * 6,
        out_specs=(raw,) * 4,
        scratch_shapes=[
            vm((1, 16, FAN), F32), vm((1, 16, FAN), F32), vm((1, 16), F32), vm((1, 16), F32),
            vm((1, 16, FAN), F32), vm((1, 16, FAN), F32), vm((2, 16, FAN), F32), dma((4,)),
            vm((NY, H, W, G), BF), vm((NY, H, W, G), BF),
            vm((NY, H, W, G), BF), vm((NY, H, W, G), BF),
            vm((2, 16, FAN), BF), vm((2, G, FAN), BF),
            vm((2, 6 * G, 4 * G), BF), vm((2, 4 * G, 6 * G), BF),
            vm((NY, PIX + 2 * W, G), BF), vm((NY, PIX + 2 * W, G), BF),
            vm((NY, PIX + 2 * W, G), BF), vm((NY, PIX + 2 * W, G), BF),
            vm((NY, PIX, G), F32), vm((1, PIX, G), F32),
            vm((2, 3 * G, 3 * G), F32),
            vm((2, NX, NZ, 16, FAN), BF), vm((2, NX, NZ, 16, FAN), BF),
            vm((2, 16, FAN), BF), vm((2, 16, FAN), BF),
            dma((2, NY, 4)), dma((2, NY)), dma((2, 2 * NX - 1)), dma((2, 3)),
            dma((2, NY, 4)), dma((2,)), dma((2, NX)), dma((2, 2)),
        ],
        compiler_params=pltpu.CompilerParams(
            collective_id=0, has_side_effects=True, vmem_limit_bytes=48 << 20
        ),
        name="block",
    )(*[pltpu.with_memory_space_constraint(v, pltpu.HBM) for v in (features, cotangent, kernel_one, kernel_two, gain_one, gain_two)])
    return pl.pallas_call(
        deliver,
        out_shape=shapes,
        in_specs=[raw] * 4,
        out_specs=(raw,) * 4,
        scratch_shapes=[dma((4,))],
        compiler_params=pltpu.CompilerParams(vmem_limit_bytes=1 << 20),
        name="deliver",
    )(*results)


def solution(mesh):
    return jax.shard_map(
        local,
        mesh=mesh,
        in_specs=(
            P("dp", "row", "col", None),
            P("dp", "row", "col", None),
            P(("row", "col"), "dp", None),
            P(("row", "col"), "dp", None),
            P(("row", "col"), "dp"),
            P(("row", "col"), "dp"),
        ),
        out_specs=(
            P("dp", "row", "col", None),
            P("dp", "row", "col", None),
            P(("row", "col"), "dp", None),
            P(("row", "col"), "dp", None),
        ),
        check_vma=False,
    )
```
